256 devices in a mesh: sens: 4 (over y), samp: 64 (over z, x, core).
Axes of the slice: x: 4, y: 4, z: 8, core: 2. Of those that a mesh axis runs over, the one named last changes fastest.
Arguments:
- slopes: bfloat16 [2, 256, 150528], P(None, 'samp', 'sens'), may hold values from -0.0625 to 0.0625
- targets: bfloat16 [2, 16384, 256], P(None, 'samp'), may hold values from -6 to 6
- reconstructor: float32 [4, 64, 32, 128, 128], P('sens', 'samp'), may hold values from -6 to 6
- foot_act: int32 [4, 64, 32], P('sens'), may hold values from 0 to 1, as said below
- foot_slope: int32 [4, 64, 32], P('sens'), may hold values from 0 to 293, as said below
- foot_count: int32 [4, 64], P('sens'), may hold values from 16 to 32, as said below
Outputs:
- fitted: float32 [4, 64, 32, 128, 128], P('sens', 'samp')
- fit_residual: bfloat16 [16384, 256], P('samp')
The draws below stay inside these ranges and needn't reach their ends.
Inputs may be any that keep to these rules, and one draw needn't show every extreme that they name: `foot_act`: slots 0 to foot_count-1 of a device are live, the rest padding (actuator block 0 and a slope block already named by slot 0); no (actuator block, slope block) pair repeats among live slots; the slope blocks of one actuator block form a run of consecutive blocks modulo 294. `foot_slope`: the live slots of one device name at most 20 distinct slope blocks; for every sens index some device names exactly 20. `foot_count`: for every sens index some device has 32 live slots.
All inputs are finite; a program needn't handle non-finite values.
Results may differ from the reference program's by a relative error of at most 0.0037.
Values may be sent and summed in bfloat16 or wider, within the bound.
A program may use at most 64 MiB of HBM per device.

```python
import jax
import jax.numpy as jnp
from jax import lax

SB = 128
ACT_DEV = 2
SGB = 294
K_MAX = 32
DIST_MAX = 20
STEPS = 2
SLOPES = 150528
ACTUATORS = 16384
SAMPLES = 256
N_SENS = 4
N_SAMP = 64


def footprint_tables(key):
    base_key = jax.random.fold_in(key, 7331)
    keys = jax.random.split(base_key, 5)
    grid_shape = (N_SENS, N_SAMP)
    first_len = jax.random.randint(keys[0], grid_shape, K_MAX // 4, K_MAX // 2 + 1)
    second_len = jax.random.randint(keys[1], grid_shape, K_MAX // 4, K_MAX // 2 + 1)
    start_block = jax.random.randint(keys[2], grid_shape, 0, SGB)
    offset = jax.random.randint(keys[3], grid_shape, 0, DIST_MAX - K_MAX // 2 + 1)
    forced = jax.random.randint(keys[4], (N_SENS,), 0, N_SAMP)
    is_forced = jnp.arange(N_SAMP)[None, :] == forced[:, None]
    first_len = jnp.where(is_forced, K_MAX // 2, first_len)
    second_len = jnp.where(is_forced, K_MAX // 2, second_len)
    offset = jnp.where(is_forced, DIST_MAX - K_MAX // 2, offset)
    slot_ids = jnp.arange(K_MAX)[None, None, :]
    first_end = first_len[:, :, None]
    in_first = slot_ids < first_end
    in_second = (slot_ids >= first_end) & (slot_ids < first_end + second_len[:, :, None])
    start_col = start_block[:, :, None]
    act_table = jnp.where(in_second, 1, 0).astype(jnp.int32)
    slope_table = jnp.where(in_first, start_col + slot_ids, jnp.where(in_second, start_col + offset[:, :, None] + slot_ids - first_end, start_col))
    slope_table = (slope_table % SGB).astype(jnp.int32)
    count_table = (first_len + second_len).astype(jnp.int32)
    return (act_table, slope_table, count_table)


def draw_foot_act(key, part):
    return footprint_tables(key)[0]


def draw_foot_slope(key, part):
    return footprint_tables(key)[1]


def draw_foot_count(key, part):
    return footprint_tables(key)[2]


def level_of(key, dims, shards, low, high):
    gain = 1.0
    for axis_at, shards_of in shards:
        steps = jax.random.uniform(jax.random.fold_in(jax.random.fold_in(key, 6), axis_at), (shards_of,), jnp.float32, low / len(shards), high / len(shards))
        gain = gain * jnp.repeat(jnp.exp(steps), dims[axis_at] // shards_of).reshape((-1,) + (1,) * (len(dims) - 1 - axis_at))
    return gain


def bell_draw(key, extent, width, most, cuts=(), dtype=jnp.bfloat16):
    entries = width * jax.random.normal(key, extent, jnp.float32)
    if cuts:
        entries = entries * level_of(key, extent, cuts, -0.22, 0.18)
    return jnp.clip(entries, -most, most).astype(dtype)


def setup_inputs(seed: int = 0) -> dict:
    key_list = jax.random.split(jax.random.key(seed), 7)
    slopes = bell_draw(key_list[0], (STEPS, SAMPLES, SLOPES), (2 * K_MAX * SB) ** -0.5, 0.0625, ((1, 64), (2, 4)))
    targets = bell_draw(key_list[1], (STEPS, ACTUATORS, SAMPLES), 1.0, 6.0, ((1, 64),))
    reconstructor = bell_draw(key_list[2], (N_SENS, N_SAMP, K_MAX, SB, SB), 1.0, 6.0, ((0, 4), (1, 64)), jnp.float32)
    foot_act = draw_foot_act(jax.random.fold_in(key_list[6], 71), 0)
    foot_slope = draw_foot_slope(jax.random.fold_in(key_list[6], 71), 0)
    foot_count = draw_foot_count(jax.random.fold_in(key_list[6], 71), 0)
    return {"slopes": slopes, "targets": targets, "reconstructor": reconstructor, "foot_act": foot_act, "foot_slope": foot_slope, "foot_count": foot_count}


def reference(slopes, targets, reconstructor, foot_act, foot_slope, foot_count):
    step_rate = K_MAX * SB / (SAMPLES + 3 * K_MAX * SB)
    live_slots = jnp.arange(K_MAX)[None, None, :] < foot_count[:, :, None]
    act_onehot = ((foot_act[:, :, None, :] == jnp.arange(ACT_DEV)[None, None, :, None])
                  & live_slots[:, :, None, :]).astype(jnp.float32)
    sens_ids = jnp.arange(N_SENS)
    weights = jnp.transpose(reconstructor, (1, 0, 2, 3, 4))
    slope_by_dev = jnp.transpose(foot_slope, (1, 0, 2))
    act_by_dev = jnp.transpose(foot_act, (1, 0, 2))
    live_by_dev = jnp.transpose(live_slots, (1, 0, 2))
    onehot_by_dev = jnp.transpose(act_onehot, (1, 0, 2, 3))
    residuals = None
    for step in range(STEPS):
        slope_blocks = slopes[step].reshape(SAMPLES, N_SENS, SGB, SB)
        target_blocks = targets[step].reshape(N_SAMP, ACT_DEV, SB, SAMPLES)

        def device_update(device_items):
            weights_dev, slope_dev, onehot_dev, live_dev, act_dev, target_dev = device_items
            picked = slope_blocks[:, sens_ids[:, None], slope_dev, :].astype(jnp.float32)
            weights_low = weights_dev.astype(jnp.bfloat16).astype(jnp.float32)
            partial_sums = jnp.einsum('skil,nskl->skin', weights_low, picked)
            prediction = jnp.einsum('sjk,skin->jin', onehot_dev, partial_sums,
                                    precision=lax.Precision.HIGHEST)
            residual = (prediction - target_dev.astype(jnp.float32)).astype(jnp.bfloat16)
            slot_residual = residual[act_dev].astype(jnp.float32)
            gradient = jnp.einsum('skin,nskl->skil', slot_residual, picked)
            updated = jnp.where(live_dev[:, :, None, None], weights_dev - step_rate * gradient, weights_dev)
            return updated, residual

        weights, residuals = lax.map(device_update, (weights, slope_by_dev, onehot_by_dev,
                                                     live_by_dev, act_by_dev, target_blocks))
    fitted = jnp.transpose(weights, (1, 0, 2, 3, 4))
    return fitted, residuals.reshape(ACTUATORS, SAMPLES)
```

```python
import functools

import jax
import jax.numpy as jnp
from jax import lax
from jax.experimental import pallas as pl
from jax.experimental.pallas import tpu as pltpu
from jax.sharding import PartitionSpec as P

MESH = pl.DeviceIdType.MESH
STEPS = 2
SB = 128
SGB = 294
K_MAX = 32
DIST = 20
ACT_DEV = 2
SAMPLES = 256
LOCAL = 4
WIDE = DIST * SB
HALF = SGB // 2
RATE = K_MAX * SB / (SAMPLES + 3 * K_MAX * SB)
OFFS = (0, -1, 1, -2, 2, -3, 3, 4)
F32 = jnp.float32
BF16 = jnp.bfloat16


def place(off):
    return OFFS.index(4 if off == -4 else off)


def kernel(slopes, targets, recon, dist_tab, int_tab, flt_tab, fitted, resid_out,
           grid0, grid1, pick0, pick1, got0, got1, mat, weights, low_t, recon_v, outbuf,
           preds, goal, perm, load_sem, zs, zr, xs, xr, ys, yr, out_sem):
    grids, picks, gots = (grid0, grid1), (pick0, pick1), (got0, got1)
    sens = lax.axis_index("sens")
    samp = lax.axis_index("samp")
    plane = samp // 8
    col = (samp % 8) // 2
    core = samp % 2
    own_q = samp % 8

    def z_dev(step):
        return (sens, (samp + 8 * step + 64) % 64)

    def q_of(e, sign):
        return ((col + sign * (e // 2) + 4) % 4) * 2 + (core + e) % 2

    def z_copy(way, t, hop, half):
        sign = -1 if way == 0 else 1
        window = pl.ds(half * HALF, HALF)
        return pltpu.make_async_remote_copy(
            src_ref=grids[t][place(sign * hop)].at[window],
            dst_ref=grids[t][place(sign * (hop + 1))].at[window],
            send_sem=zs.at[way, t, hop, half],
            recv_sem=zr.at[way, t, hop, half],
            device_id=z_dev(-sign),
            device_id_type=MESH,
        )

    def x_copy(t, r, e):
        return pltpu.make_async_remote_copy(
            src_ref=picks[t][r].at[e],
            dst_ref=gots[t].at[r, own_q],
            send_sem=xs.at[t, r, e],
            recv_sem=xr.at[t, r, e],
            device_id=(sens, plane * 8 + q_of(e, 1)),
            device_id_type=MESH,
        )

    def x_arrival(t, r, e):
        return pltpu.make_async_remote_copy(
            src_ref=picks[t][r].at[e],
            dst_ref=gots[t].at[r, q_of(e, -1)],
            send_sem=xs.at[t, r, e],
            recv_sem=xr.at[t, r, e],
            device_id=(sens, plane * 8 + q_of(e, -1)),
            device_id_type=MESH,
        )

    def y_copy(t, e):
        return pltpu.make_async_remote_copy(
            src_ref=preds.at[t, sens],
            dst_ref=preds.at[t, sens],
            send_sem=ys.at[t, e - 1],
            recv_sem=yr.at[t, e - 1],
            device_id=((sens + e) % 4, samp),
            device_id_type=MESH,
        )

    def y_arrival(t, e):
        other = (sens - e + 4) % 4
        return pltpu.make_async_remote_copy(
            src_ref=preds.at[t, other],
            dst_ref=preds.at[t, other],
            send_sem=ys.at[t, e - 1],
            recv_sem=yr.at[t, e - 1],
            device_id=(other, samp),
            device_id_type=MESH,
        )

    def forward(t, hop, half):
        for way in range(2):
            z_copy(way, t, hop - 1, half).wait_recv()
            if hop < 3 or half == way:
                z_copy(way, t, hop, half).start()

    def pick(t, r):
        src = grids[t][r]

        def one(e, to):
            row = plane * 8 + q_of(e, 1)
            for d in range(DIST):
                to[:, d * SB:(d + 1) * SB] = src[dist_tab[row, d]]

        one(0, gots[t].at[r, own_q])

        @pl.loop(1, 8)
        def _(e):
            one(e, picks[t][r].at[e])

    def send_picked(t, r):
        for e in range(1, 8):
            x_copy(t, r, e).start()

    def assemble(t, r):
        for e in range(1, 8):
            x_arrival(t, r, e).wait_recv()
        for half in range(2):
            piece = jnp.concatenate([gots[t][r, half * 4 + q] for q in range(4)], axis=0)
            mat[t, pl.ds(r * 32 + half * 16, 16), :] = piece

    def low_weights():
        @pl.loop(0, DIST)
        def _(d):
            for j in range(ACT_DEV):
                block = weights[j * DIST + d].astype(BF16)
                low_t[pl.ds(pl.multiple_of(d * SB, SB), SB), j * SB:(j + 1) * SB] = block.T

    def predict(t):
        part = jnp.dot(mat[t], low_t[...], preferred_element_type=F32)
        preds[t, sens] = part.astype(BF16)

    def residual(t):
        total = preds[t, 0].astype(F32)
        for s in range(1, 4):
            total = total + preds[t, s].astype(F32)
        return (total - goal[t]).astype(BF16).T

    def gradient(t, resid):
        @pl.loop(0, DIST // 2)
        def _(g):
            cols = pl.ds(pl.multiple_of(g * 2 * SB, 2 * SB), 2 * SB)
            grad = jnp.dot(resid, mat[t, :, cols], preferred_element_type=F32)
            for j in range(ACT_DEV):
                for side in range(2):
                    at = j * DIST + g * 2 + side
                    scale = RATE * flt_tab[at]
                    weights[at] = weights[at] - scale * grad[j * SB:(j + 1) * SB, side * SB:(side + 1) * SB]

    own_loads = [pltpu.make_async_copy(slopes.at[t], grids[t][0], load_sem.at[t]) for t in range(STEPS)]
    recon_load = pltpu.make_async_copy(recon, recon_v, load_sem.at[2])
    for load in own_loads:
        load.start()
    recon_load.start()

    barrier = pltpu.get_barrier_semaphore()
    for step in (1, -1):
        pl.semaphore_signal(barrier, inc=1, device_id=z_dev(step), device_id_type=MESH)
    for e in range(1, 8):
        pl.semaphore_signal(barrier, inc=1, device_id=(sens, plane * 8 + q_of(e, 1)), device_id_type=MESH)
    for e in range(1, 4):
        pl.semaphore_signal(barrier, inc=1, device_id=((sens + e) % 4, samp), device_id_type=MESH)
    pl.semaphore_wait(barrier, 12)

    own_loads[0].wait()
    for half in range(2):
        for way in range(2):
            z_copy(way, 0, 0, half).start()
    own_loads[1].wait()
    pick(0, 0)
    send_picked(0, 0)

    recon_load.wait()

    @pl.loop(0, ACT_DEV * DIST)
    def _(at):
        weights[at] = recon_v[int_tab[at]] * flt_tab[at]

    low_weights()

    rows = lax.broadcasted_iota(jnp.int32, (SAMPLES, SAMPLES), 0)
    cols = lax.broadcasted_iota(jnp.int32, (SAMPLES, SAMPLES), 1)
    off = jnp.zeros_like(rows)
    for r in range(8):
        off = jnp.where(rows // 32 == r, (plane + OFFS[r] + 8) % 8, off)
    perm[...] = jnp.where(cols == off * 32 + rows % 32, 1.0, 0.0).astype(BF16)
    for t in range(STEPS):
        goal[t] = lax.dot_general(perm[...], targets[t], (((1,), (1,)), ((), ())),
                                  preferred_element_type=F32)

    for hop in range(1, 4):
        for half in range(2):
            forward(0, hop, half)
        if hop == 3:
            for half in range(2):
                for way in range(2):
                    z_copy(way, 1, 0, half).start()
        for sign in (-1, 1):
            pick(0, place(sign * hop))
            send_picked(0, place(sign * hop))
        if hop > 1:
            for r in ((0, 1, 2) if hop == 2 else (3, 4)):
                assemble(0, r)
    pick(1, 0)
    send_picked(1, 0)
    for way in range(2):
        z_copy(way, 0, 3, way).wait_recv()
    pick(0, 7)
    send_picked(0, 7)
    assemble(0, 5)
    assemble(0, 6)
    forward(1, 1, 0)
    assemble(0, 7)
    predict(0)
    for e in range(1, 4):
        y_copy(0, e).start()
    forward(1, 1, 1)
    for r in (1, 2):
        pick(1, r)
        send_picked(1, r)
    assemble(1, 0)
    for e in range(1, 4):
        y_arrival(0, e).wait_recv()
    gradient(0, residual(0))
    forward(1, 2, 0)
    low_weights()
    forward(1, 2, 1)
    for r in (3, 4):
        pick(1, r)
        send_picked(1, r)
    assemble(1, 1)
    assemble(1, 2)
    for half in range(2):
        forward(1, 3, half)
    for r in (5, 6):
        pick(1, r)
        send_picked(1, r)
    assemble(1, 3)
    assemble(1, 4)
    for way in range(2):
        z_copy(way, 1, 3, way).wait_recv()
    pick(1, 7)
    send_picked(1, 7)
    for r in (5, 6, 7):
        assemble(1, r)
    predict(1)
    for e in range(1, 4):
        y_copy(1, e).start()
    for e in range(1, 4):
        y_arrival(1, e).wait_recv()
    resid = residual(1)
    gradient(1, resid)

    outs = []
    for c in range(4):
        @pl.loop(c * 8, (c + 1) * 8)
        def _(k):
            fresh = weights[int_tab[ACT_DEV * DIST + k]]
            live = flt_tab[ACT_DEV * DIST + k]
            outbuf[k] = fresh * live + recon_v[k] * (1.0 - live)

        out = pltpu.make_async_copy(outbuf.at[pl.ds(c * 8, 8)], fitted.at[pl.ds(c * 8, 8)], out_sem.at[c])
        out.start()
        outs.append(out)
    resid_out[...] = jnp.dot(resid, perm[...], preferred_element_type=F32).astype(BF16)

    for t in range(STEPS):
        for hop in range(4):
            for half in range(2):
                for way in range(2):
                    if hop < 3 or half == way:
                        z_copy(way, t, hop, half).wait_send()
        for r in range(8):
            for e in range(1, 8):
                x_copy(t, r, e).wait_send()
        for e in range(1, 4):
            y_copy(t, e).wait_send()
    for out in outs:
        out.wait()


def tables(foot_act, foot_slope, foot_count, own):
    slot = jnp.arange(K_MAX)
    same = foot_slope[:, :, None] == foot_slope[:, None, :]
    first = jnp.min(jnp.where(same, slot[None, None, :], K_MAX), axis=2)
    fresh = first == slot[None, :]
    rank = jnp.sum(fresh[:, None, :] & (slot[None, None, :] < first[:, :, None]), axis=2)
    at_rank = fresh[:, None, :] & (rank[:, None, :] == jnp.arange(DIST)[None, :, None])
    dist_tab = jnp.sum(jnp.where(at_rank, foot_slope[:, None, :], 0), axis=2)
    act = lax.dynamic_index_in_dim(foot_act, own, 0, keepdims=False)
    live = slot < lax.dynamic_index_in_dim(foot_count, own, 0, keepdims=False)
    pos = act * DIST + lax.dynamic_index_in_dim(rank, own, 0, keepdims=False)
    holds = live[None, :] & (pos[None, :] == jnp.arange(ACT_DEV * DIST)[:, None])
    slot_of = jnp.sum(jnp.where(holds, slot[None, :], 0), axis=1)
    int_tab = jnp.concatenate([slot_of, pos]).astype(jnp.int32)
    flt_tab = jnp.concatenate([jnp.any(holds, axis=1), live]).astype(F32)
    return dist_tab.astype(jnp.int32), int_tab, flt_tab


def per_device(slopes, targets, reconstructor, foot_act, foot_slope, foot_count):
    own = lax.axis_index("samp")
    dist_tab, int_tab, flt_tab = tables(foot_act[0], foot_slope[0], foot_count[0], own)
    recon = reconstructor[0, 0]
    slopes = slopes.reshape(STEPS, LOCAL, SGB, SB).transpose(0, 2, 1, 3)
    vmem, smem, anywhere = (pl.BlockSpec(memory_space=m) for m in (pltpu.VMEM, pltpu.SMEM, pl.ANY))
    grid_set = [pltpu.VMEM((SGB, LOCAL, SB), BF16)] * 8
    pick_set = [pltpu.VMEM((8, LOCAL, WIDE), BF16)] * 8
    dma = pltpu.SemaphoreType.DMA
    fitted, resid = pl.pallas_call(
        kernel,
        out_shape=(jax.ShapeDtypeStruct(recon.shape, F32),
                   jax.ShapeDtypeStruct((ACT_DEV * SB, SAMPLES), BF16)),
        in_specs=[anywhere, vmem, anywhere, smem, smem, smem],
        out_specs=(anywhere, vmem),
        scratch_shapes=[
            grid_set, grid_set, pick_set, pick_set,
            pltpu.VMEM((8, 8, LOCAL, WIDE), BF16),
            pltpu.VMEM((8, 8, LOCAL, WIDE), BF16),
            pltpu.VMEM((STEPS, SAMPLES, WIDE), BF16),
            pltpu.VMEM((ACT_DEV * DIST, SB, SB), F32),
            pltpu.VMEM((WIDE, ACT_DEV * SB), BF16),
            pltpu.VMEM((K_MAX, SB, SB), F32),
            pltpu.VMEM((K_MAX, SB, SB), F32),
            pltpu.VMEM((STEPS, 4, SAMPLES, ACT_DEV * SB), BF16),
            pltpu.VMEM((STEPS, SAMPLES, ACT_DEV * SB), F32),
            pltpu.VMEM((SAMPLES, SAMPLES), BF16),
            dma((3,)),
            dma((2, STEPS, 4, 2)), dma((2, STEPS, 4, 2)),
            dma((STEPS, 8, 8)), dma((STEPS, 8, 8)),
            dma((STEPS, 3)), dma((STEPS, 3)),
            dma((4,)),
        ],
        compiler_params=pltpu.CompilerParams(
            collective_id=0, has_side_effects=True, vmem_limit_bytes=60 * 1024 * 1024),
    )(slopes, targets, recon, dist_tab, int_tab, flt_tab)
    return fitted[None, None], resid


def solution(mesh):
    return jax.shard_map(
        per_device,
        mesh=mesh,
        in_specs=(
            P(None, "samp", "sens"),
            P(None, "samp", None),
            P("sens", "samp", None, None, None),
            P("sens", None, None),
            P("sens", None, None),
            P("sens", None),
        ),
        out_specs=(P("sens", "samp", None, None, None), P("samp", None)),
        check_vma=False,
    )
```

```python
import functools

import jax
import jax.numpy as jnp
from jax import lax
from jax.experimental import pallas as pl
from jax.experimental.pallas import tpu as pltpu
from jax.sharding import PartitionSpec as P

MESH = pl.DeviceIdType.MESH
STEPS = 2
SB = 128
SGB = 294
K_MAX = 32
DIST = 20
ACT_DEV = 2
SAMPLES = 256
LOCAL = 4
WIDE = DIST * SB
HALF = SGB // 2
RATE = K_MAX * SB / (SAMPLES + 3 * K_MAX * SB)
OFFS = (0, -1, 1, -2, 2, -3, 3, 4)
F32 = jnp.float32
BF16 = jnp.bfloat16


def place(off):
    return OFFS.index(4 if off == -4 else off)


CHUNKS = ((0, 160), (160, 224), (224, 256))
ROW_POS = 24
ROW_SLOT = ROW_POS + K_MAX
ROW_MASK = ROW_SLOT + ACT_DEV * DIST
ROW_LIVE = ROW_MASK + ACT_DEV * DIST
TAB_ROWS = ROW_LIVE + K_MAX


def fill_tables(act, slope, count, tab):
    n = slope.shape[1]
    slot = lax.broadcasted_iota(jnp.int32, (K_MAX, n), 0)
    blocks = slope[...]
    first = jnp.full((K_MAX, n), K_MAX, jnp.int32)
    for k in reversed(range(K_MAX)):
        first = jnp.where(blocks == blocks[k:k + 1], k, first)
    fresh = jnp.where(first == slot, 1, 0)
    rank = jnp.zeros((K_MAX, n), jnp.int32)
    for k in range(K_MAX):
        rank = rank + jnp.where(first > k, fresh[k:k + 1], 0)
    pos = act[...] * DIST + rank
    live = jnp.where(slot < count[...], 1, 0)
    order = lax.broadcasted_iota(jnp.int32, (ROW_POS, n), 0)
    place_of = lax.broadcasted_iota(jnp.int32, (ACT_DEV * DIST, n), 0)
    held = jnp.zeros((ROW_POS, n), jnp.int32)
    slot_of = jnp.zeros((ACT_DEV * DIST, n), jnp.int32)
    mask = jnp.zeros((ACT_DEV * DIST, n), jnp.int32)
    for k in range(K_MAX):
        held = held + jnp.where(order == rank[k:k + 1], blocks[k:k + 1] * fresh[k:k + 1], 0)
        hit = jnp.where(place_of == pos[k:k + 1], live[k:k + 1], 0)
        slot_of = slot_of + hit * k
        mask = mask + hit
    tab[0:ROW_POS, :] = held
    tab[ROW_POS:ROW_SLOT, :] = pos
    tab[ROW_SLOT:ROW_MASK, :] = slot_of
    tab[ROW_MASK:ROW_LIVE, :] = mask
    tab[ROW_LIVE:TAB_ROWS, :] = live


def kernel(slopes, targets, recon, act, slope, count, fitted, resid_out,
           tab_v, tab, grid0, grid1, pick0, pick1, got0, got1, mat, weights, low_t, recon_v, outbuf,
           preds, goal, perm, resid, load_sem, zs, zr, xs, xr, ys, yr, out_sem):
    grids, picks, gots = (grid0, grid1), (pick0, pick1), (got0, got1)
    sens = lax.axis_index("sens")
    samp = lax.axis_index("samp")
    plane = samp // 8
    col = (samp % 8) // 2
    core = samp % 2
    own_q = samp % 8

    def z_dev(step):
        return (sens, (samp + 8 * step + 64) % 64)

    def q_of(e, sign):
        return ((col + sign * (e // 2) + 4) % 4) * 2 + (core + e) % 2

    def z_copy(way, t, hop, half):
        sign = -1 if way == 0 else 1
        window = pl.ds(half * HALF, HALF)
        return pltpu.make_async_remote_copy(
            src_ref=grids[t][place(sign * hop)].at[window],
            dst_ref=grids[t][place(sign * (hop + 1))].at[window],
            send_sem=zs.at[way, t, hop, half],
            recv_sem=zr.at[way, t, hop, half],
            device_id=z_dev(-sign),
            device_id_type=MESH,
        )

    def x_copy(t, r, e):
        return pltpu.make_async_remote_copy(
            src_ref=picks[t][r].at[e],
            dst_ref=gots[t].at[r, own_q],
            send_sem=xs.at[t, r, e],
            recv_sem=xr.at[t, r, e],
            device_id=(sens, plane * 8 + q_of(e, 1)),
            device_id_type=MESH,
        )

    def x_arrival(t, r, e):
        return pltpu.make_async_remote_copy(
            src_ref=picks[t][r].at[e],
            dst_ref=gots[t].at[r, q_of(e, -1)],
            send_sem=xs.at[t, r, e],
            recv_sem=xr.at[t, r, e],
            device_id=(sens, plane * 8 + q_of(e, -1)),
            device_id_type=MESH,
        )

    def y_copy(t, c, e):
        rows = pl.ds(CHUNKS[c][0], CHUNKS[c][1] - CHUNKS[c][0])
        return pltpu.make_async_remote_copy(
            src_ref=preds.at[t, sens, rows],
            dst_ref=preds.at[t, sens, rows],
            send_sem=ys.at[t, c, e - 1],
            recv_sem=yr.at[t, c, e - 1],
            device_id=((sens + e) % 4, samp),
            device_id_type=MESH,
        )

    def y_arrival(t, c, e):
        other = (sens - e + 4) % 4
        rows = pl.ds(CHUNKS[c][0], CHUNKS[c][1] - CHUNKS[c][0])
        return pltpu.make_async_remote_copy(
            src_ref=preds.at[t, other, rows],
            dst_ref=preds.at[t, other, rows],
            send_sem=ys.at[t, c, e - 1],
            recv_sem=yr.at[t, c, e - 1],
            device_id=(other, samp),
            device_id_type=MESH,
        )

    def forward(t, hop, half):
        for way in range(2):
            z_copy(way, t, hop - 1, half).wait_recv()
            if hop < 3 or half == way:
                z_copy(way, t, hop, half).start()

    def pick(t, r):
        src = grids[t][r]

        def one(e, to):
            row = plane * 8 + q_of(e, 1)
            for d in range(DIST):
                to[:, d * SB:(d + 1) * SB] = src[tab[d, row]]

        one(0, gots[t].at[r, own_q])

        @pl.loop(1, 8)
        def _(e):
            one(e, picks[t][r].at[e])

    def send_picked(t, r):
        for e in range(1, 8):
            x_copy(t, r, e).start()

    def assemble(t, r):
        for e in range(1, 8):
            x_arrival(t, r, e).wait_recv()
        for half in range(2):
            piece = jnp.concatenate([gots[t][r, half * 4 + q] for q in range(4)], axis=0)
            mat[t, pl.ds(r * 32 + half * 16, 16), :] = piece

    def low_weights():
        @pl.loop(0, DIST)
        def _(d):
            for j in range(ACT_DEV):
                block = weights[j * DIST + d].astype(BF16)
                low_t[pl.ds(pl.multiple_of(d * SB, SB), SB), j * SB:(j + 1) * SB] = block.T

    def predict(t, c):
        rows = slice(*CHUNKS[c])
        part = jnp.dot(mat[t, rows], low_t[...], preferred_element_type=F32)
        preds[t, sens, rows] = part.astype(BF16)
        for e in range(1, 4):
            y_copy(t, c, e).start()

    def residual(t, c):
        rows = slice(*CHUNKS[c])
        for e in range(1, 4):
            y_arrival(t, c, e).wait_recv()
        total = preds[t, 0, rows].astype(F32)
        for s in range(1, 4):
            total = total + preds[t, s, rows].astype(F32)
        resid[rows] = (total - goal[t, rows]).astype(BF16)

    def gradient(t, lo, hi):
        turned = resid[lo:hi].T

        @pl.loop(0, DIST // 2)
        def _(g):
            cols = pl.ds(pl.multiple_of(g * 2 * SB, 2 * SB), 2 * SB)
            grad = jnp.dot(turned, mat[t, lo:hi, cols], preferred_element_type=F32)
            for j in range(ACT_DEV):
                for side in range(2):
                    at = j * DIST + g * 2 + side
                    scale = RATE * tab[ROW_MASK + at, samp].astype(F32)
                    weights[at] = weights[at] - scale * grad[j * SB:(j + 1) * SB, side * SB:(side + 1) * SB]

    own_loads = [pltpu.make_async_copy(slopes.at[t], grids[t][0], load_sem.at[t]) for t in range(STEPS)]
    recon_load = pltpu.make_async_copy(recon, recon_v, load_sem.at[2])
    for load in own_loads:
        load.start()
    recon_load.start()

    barrier = pltpu.get_barrier_semaphore()
    for step in (1, -1):
        pl.semaphore_signal(barrier, inc=1, device_id=z_dev(step), device_id_type=MESH)
    for e in range(1, 8):
        pl.semaphore_signal(barrier, inc=1, device_id=(sens, plane * 8 + q_of(e, 1)), device_id_type=MESH)
    for e in range(1, 4):
        pl.semaphore_signal(barrier, inc=1, device_id=((sens + e) % 4, samp), device_id_type=MESH)
    pl.semaphore_wait(barrier, 12)

    own_loads[0].wait()
    for half in range(2):
        for way in range(2):
            z_copy(way, 0, 0, half).start()
    fill_tables(act, slope, count, tab_v)
    tab_load = pltpu.make_async_copy(tab_v, tab, load_sem.at[3])
    tab_load.start()
    own_loads[1].wait()
    tab_load.wait()
    pick(0, 0)
    send_picked(0, 0)

    recon_load.wait()

    @pl.loop(0, ACT_DEV * DIST)
    def _(at):
        weights[at] = recon_v[tab[ROW_SLOT + at, samp]] * tab[ROW_MASK + at, samp].astype(F32)

    low_weights()

    rows = lax.broadcasted_iota(jnp.int32, (SAMPLES, SAMPLES), 0)
    cols = lax.broadcasted_iota(jnp.int32, (SAMPLES, SAMPLES), 1)
    off = jnp.zeros_like(rows)
    for r in range(8):
        off = jnp.where(rows // 32 == r, (plane + OFFS[r] + 8) % 8, off)
    perm[...] = jnp.where(cols == off * 32 + rows % 32, 1.0, 0.0).astype(BF16)
    for t in range(STEPS):
        goal[t] = lax.dot_general(perm[...], targets[t], (((1,), (1,)), ((), ())),
                                  preferred_element_type=F32)

    for hop in range(1, 4):
        for half in range(2):
            forward(0, hop, half)
        if hop == 3:
            for half in range(2):
                for way in range(2):
                    z_copy(way, 1, 0, half).start()
        for sign in (-1, 1):
            pick(0, place(sign * hop))
            send_picked(0, place(sign * hop))
        if hop > 1:
            for r in ((0, 1, 2) if hop == 2 else (3, 4)):
                assemble(0, r)
    pick(1, 0)
    send_picked(1, 0)
    for way in range(2):
        z_copy(way, 0, 3, way).wait_recv()
    pick(0, 7)
    send_picked(0, 7)
    predict(0, 0)
    assemble(0, 5)
    assemble(0, 6)
    forward(1, 1, 0)
    predict(0, 1)
    assemble(0, 7)
    predict(0, 2)
    forward(1, 1, 1)
    for r in (1, 2):
        pick(1, r)
        send_picked(1, r)
    assemble(1, 0)
    for c in range(3):
        residual(0, c)
    gradient(0, 0, SAMPLES)
    forward(1, 2, 0)
    low_weights()
    forward(1, 2, 1)
    for r in (3, 4):
        pick(1, r)
        send_picked(1, r)
    assemble(1, 1)
    assemble(1, 2)
    for half in range(2):
        forward(1, 3, half)
    for r in (5, 6):
        pick(1, r)
        send_picked(1, r)
    assemble(1, 3)
    assemble(1, 4)
    predict(1, 0)
    for way in range(2):
        z_copy(way, 1, 3, way).wait_recv()
    pick(1, 7)
    send_picked(1, 7)
    assemble(1, 5)
    assemble(1, 6)
    predict(1, 1)
    residual(1, 0)
    gradient(1, *CHUNKS[0])
    assemble(1, 7)
    predict(1, 2)
    residual(1, 1)
    residual(1, 2)
    gradient(1, CHUNKS[1][0], SAMPLES)

    outs = []
    for c in range(4):
        @pl.loop(c * 8, (c + 1) * 8)
        def _(k):
            fresh = weights[tab[ROW_POS + k, samp]]
            live = tab[ROW_LIVE + k, samp].astype(F32)
            outbuf[k] = fresh * live + recon_v[k] * (1.0 - live)

        out = pltpu.make_async_copy(outbuf.at[pl.ds(c * 8, 8)], fitted.at[pl.ds(c * 8, 8)], out_sem.at[c])
        out.start()
        outs.append(out)
    resid_out[...] = jnp.dot(resid[...].T, perm[...], preferred_element_type=F32).astype(BF16)

    for t in range(STEPS):
        for hop in range(4):
            for half in range(2):
                for way in range(2):
                    if hop < 3 or half == way:
                        z_copy(way, t, hop, half).wait_send()
        for r in range(8):
            for e in range(1, 8):
                x_copy(t, r, e).wait_send()
        for c in range(3):
            for e in range(1, 4):
                y_copy(t, c, e).wait_send()
    for out in outs:
        out.wait()


def per_device(slopes, targets, reconstructor, foot_act, foot_slope, foot_count):
    recon = reconstructor[0, 0]
    slopes = slopes.reshape(STEPS, LOCAL, SGB, SB).transpose(0, 2, 1, 3)
    vmem, anywhere = (pl.BlockSpec(memory_space=m) for m in (pltpu.VMEM, pl.ANY))
    grid_set = [pltpu.VMEM((SGB, LOCAL, SB), BF16)] * 8
    pick_set = [pltpu.VMEM((8, LOCAL, WIDE), BF16)] * 8
    dma = pltpu.SemaphoreType.DMA
    n_samp = foot_count.shape[1]
    fitted, resid = pl.pallas_call(
        kernel,
        out_shape=(jax.ShapeDtypeStruct(recon.shape, F32),
                   jax.ShapeDtypeStruct((ACT_DEV * SB, SAMPLES), BF16)),
        in_specs=[anywhere, vmem, anywhere, vmem, vmem, vmem],
        out_specs=(anywhere, vmem),
        scratch_shapes=[
            pltpu.VMEM((TAB_ROWS, n_samp), jnp.int32),
            pltpu.SMEM((TAB_ROWS, n_samp), jnp.int32),
            grid_set, grid_set, pick_set, pick_set,
            pltpu.VMEM((8, 8, LOCAL, WIDE), BF16),
            pltpu.VMEM((8, 8, LOCAL, WIDE), BF16),
            pltpu.VMEM((STEPS, SAMPLES, WIDE), BF16),
            pltpu.VMEM((ACT_DEV * DIST, SB, SB), F32),
            pltpu.VMEM((WIDE, ACT_DEV * SB), BF16),
            pltpu.VMEM((K_MAX, SB, SB), F32),
            pltpu.VMEM((K_MAX, SB, SB), F32),
            pltpu.VMEM((STEPS, 4, SAMPLES, ACT_DEV * SB), BF16),
            pltpu.VMEM((STEPS, SAMPLES, ACT_DEV * SB), F32),
            pltpu.VMEM((SAMPLES, SAMPLES), BF16),
            pltpu.VMEM((SAMPLES, ACT_DEV * SB), BF16),
            dma((4,)),
            dma((2, STEPS, 4, 2)), dma((2, STEPS, 4, 2)),
            dma((STEPS, 8, 8)), dma((STEPS, 8, 8)),
            dma((STEPS, 3, 3)), dma((STEPS, 3, 3)),
            dma((4,)),
        ],
        compiler_params=pltpu.CompilerParams(
            collective_id=0, has_side_effects=True, vmem_limit_bytes=60 * 1024 * 1024),
    )(slopes, targets, recon, foot_act[0].T, foot_slope[0].T, foot_count)
    return fitted[None, None], resid


def solution(mesh):
    return jax.shard_map(
        per_device,
        mesh=mesh,
        in_specs=(
            P(None, "samp", "sens"),
            P(None, "samp", None),
            P("sens", "samp", None, None, None),
            P("sens", None, None),
            P("sens", None, None),
            P("sens", None),
        ),
        out_specs=(P("sens", "samp", None, None, None), P("samp", None)),
        check_vma=False,
    )
```

```python
import functools

import jax
import jax.numpy as jnp
from jax import lax
from jax.experimental import pallas as pl
from jax.experimental.pallas import tpu as pltpu
from jax.sharding import PartitionSpec as P

MESH = pl.DeviceIdType.MESH
STEPS = 2
SB = 128
SGB = 294
K_MAX = 32
DIST = 20
ACT_DEV = 2
SAMPLES = 256
LOCAL = 4
WIDE = DIST * SB
HALF = SGB // 2
RATE = K_MAX * SB / (SAMPLES + 3 * K_MAX * SB)
OFFS = (0, -1, 1, -2, 2, -3, 3, 4)
F32 = jnp.float32
BF16 = jnp.bfloat16


def place(off):
    return OFFS.index(4 if off == -4 else off)


CHUNKS = ((0, 160), (160, 224), (224, 256))
ROW_POS = 24
ROW_SLOT = ROW_POS + K_MAX
ROW_MASK = ROW_SLOT + ACT_DEV * DIST
ROW_LIVE = ROW_MASK + ACT_DEV * DIST
TAB_ROWS = ROW_LIVE + K_MAX


def fill_tables(act, slope, count, tab):
    n = slope.shape[1]
    slot = lax.broadcasted_iota(jnp.int32, (K_MAX, n), 0)
    blocks = slope[...]
    first = jnp.full((K_MAX, n), K_MAX, jnp.int32)
    for k in reversed(range(K_MAX)):
        first = jnp.where(blocks == blocks[k:k + 1], k, first)
    fresh = jnp.where(first == slot, 1, 0)
    rank = jnp.zeros((K_MAX, n), jnp.int32)
    for k in range(K_MAX):
        rank = rank + jnp.where(first > k, fresh[k:k + 1], 0)
    pos = act[...] * DIST + rank
    live = jnp.where(slot < count[...], 1, 0)
    order = lax.broadcasted_iota(jnp.int32, (ROW_POS, n), 0)
    place_of = lax.broadcasted_iota(jnp.int32, (ACT_DEV * DIST, n), 0)
    held = jnp.zeros((ROW_POS, n), jnp.int32)
    slot_of = jnp.zeros((ACT_DEV * DIST, n), jnp.int32)
    mask = jnp.zeros((ACT_DEV * DIST, n), jnp.int32)
    for k in range(K_MAX):
        held = held + jnp.where(order == rank[k:k + 1], blocks[k:k + 1] * fresh[k:k + 1], 0)
        hit = jnp.where(place_of == pos[k:k + 1], live[k:k + 1], 0)
        slot_of = slot_of + hit * k
        mask = mask + hit
    tab[0:ROW_POS, :] = held
    tab[ROW_POS:ROW_SLOT, :] = pos
    tab[ROW_SLOT:ROW_MASK, :] = slot_of
    tab[ROW_MASK:ROW_LIVE, :] = mask
    tab[ROW_LIVE:TAB_ROWS, :] = live


def sample_order(plane):
    rows = lax.broadcasted_iota(jnp.int32, (SAMPLES, SAMPLES), 0)
    cols = lax.broadcasted_iota(jnp.int32, (SAMPLES, SAMPLES), 1)
    off = jnp.zeros_like(rows)
    for r in range(8):
        off = jnp.where(rows // 32 == r, (plane + OFFS[r] + 8) % 8, off)
    return jnp.where(cols == off * 32 + rows % 32, 1.0, 0.0).astype(BF16)


def kernel(slopes, targets, recon, act, slope, count, base_out, tail_out, resid, tab_out,
           tab_v, tab, grid0, grid1, pick0, pick1, far_out, far_in, last_out, last_mid, last_in,
           got0, got1, mat, weights, low_t, recon_v, base,
           preds, goal, perm, load_sem, zs, zr, xs, xr, ys, yr, out_sem):
    grids, picks, gots = (grid0, grid1), (pick0, pick1), (got0, got1)
    sens = lax.axis_index("sens")
    samp = lax.axis_index("samp")
    plane = samp // 8
    col = (samp % 8) // 2
    core = samp % 2
    own_q = samp % 8

    def z_dev(step):
        return (sens, (samp + 8 * step + 64) % 64)

    def q_of(e, sign):
        return ((col + sign * (e // 2) + 4) % 4) * 2 + (core + e) % 2

    def z_copy(way, t, hop, half):
        sign = -1 if way == 0 else 1
        window = pl.ds(half * HALF, HALF)
        return pltpu.make_async_remote_copy(
            src_ref=grids[t][place(sign * hop)].at[window],
            dst_ref=grids[t][place(sign * (hop + 1))].at[window],
            send_sem=zs.at[way, t, hop, half],
            recv_sem=zr.at[way, t, hop, half],
            device_id=z_dev(-sign),
            device_id_type=MESH,
        )

    def far_copy(way, t, half):
        rows = pl.ds(half * 4, 4)
        return pltpu.make_async_remote_copy(
            src_ref=far_out[t][way].at[rows],
            dst_ref=far_in[t][way].at[rows],
            send_sem=zs.at[way, t, 2, half],
            recv_sem=zr.at[way, t, 2, half],
            device_id=z_dev(1 - 2 * way),
            device_id_type=MESH,
        )

    def last_copy(way, t, hop):
        return pltpu.make_async_remote_copy(
            src_ref=(last_out if hop == 0 else last_mid)[t][way],
            dst_ref=last_mid[t][way] if hop == 0 else last_in[t].at[pl.ds(way * 4, 4)],
            send_sem=zs.at[way, t, 3, hop],
            recv_sem=zr.at[way, t, 3, hop],
            device_id=z_dev(1 - 2 * way),
            device_id_type=MESH,
        )

    def x_source(t, r, e):
        if r < 5:
            return picks[t][r].at[e]
        return (last_in[t] if r == 7 else far_in[t][r - 5]).at[q_of(e, 1)]

    def x_copy(t, r, e):
        return pltpu.make_async_remote_copy(
            src_ref=x_source(t, r, e),
            dst_ref=gots[t].at[r, own_q],
            send_sem=xs.at[t, r, e],
            recv_sem=xr.at[t, r, e],
            device_id=(sens, plane * 8 + q_of(e, 1)),
            device_id_type=MESH,
        )

    def x_arrival(t, r, e):
        return pltpu.make_async_remote_copy(
            src_ref=x_source(t, r, e),
            dst_ref=gots[t].at[r, q_of(e, -1)],
            send_sem=xs.at[t, r, e],
            recv_sem=xr.at[t, r, e],
            device_id=(sens, plane * 8 + q_of(e, -1)),
            device_id_type=MESH,
        )

    def y_copy(t, c, e):
        rows = pl.ds(CHUNKS[c][0], CHUNKS[c][1] - CHUNKS[c][0])
        return pltpu.make_async_remote_copy(
            src_ref=preds.at[t, sens, rows],
            dst_ref=preds.at[t, sens, rows],
            send_sem=ys.at[t, c, e - 1],
            recv_sem=yr.at[t, c, e - 1],
            device_id=((sens + e) % 4, samp),
            device_id_type=MESH,
        )

    def y_arrival(t, c, e):
        other = (sens - e + 4) % 4
        rows = pl.ds(CHUNKS[c][0], CHUNKS[c][1] - CHUNKS[c][0])
        return pltpu.make_async_remote_copy(
            src_ref=preds.at[t, other, rows],
            dst_ref=preds.at[t, other, rows],
            send_sem=ys.at[t, c, e - 1],
            recv_sem=yr.at[t, c, e - 1],
            device_id=(other, samp),
            device_id_type=MESH,
        )

    def forward(t, half):
        for way in range(2):
            z_copy(way, t, 0, half).wait_recv()
            z_copy(way, t, 1, half).start()

    def pick_one(src, row, to):
        for d in range(DIST):
            to[:, d * SB:(d + 1) * SB] = src[tab[d, row]]

    def pick(t, r):
        pick_one(grids[t][r], samp, gots[t].at[r, own_q])

        @pl.loop(1, 8)
        def _(e):
            pick_one(grids[t][r], plane * 8 + q_of(e, 1), picks[t][r].at[e])

        for e in range(1, 8):
            x_copy(t, r, e).start()

    def pick_far(t):
        for half in range(2):
            for way in range(2):
                z_copy(way, t, 1, half).wait_recv()
        for way in range(2):
            ahead = (plane + 2 - 4 * way + 8) % 8 * 8 + way * 4

            @pl.loop(0, 4)
            def _(q):
                pick_one(grids[t][3 + way], ahead + q, last_out[t][way].at[q])

            last_copy(way, t, 0).start()
        for half in range(2):
            for way in range(2):
                ahead = (plane + 1 - 2 * way + 8) % 8 * 8

                @pl.loop(half * 4, half * 4 + 4)
                def _(q):
                    pick_one(grids[t][3 + way], ahead + q, far_out[t][way].at[q])

                far_copy(way, t, half).start()

    def pass_last(t):
        for way in range(2):
            last_copy(way, t, 0).wait_recv()
            last_copy(way, t, 1).start()

    def relay_far(t):
        for way in range(2):
            for half in range(2):
                far_copy(way, t, half).wait_recv()
            for e in range(1, 8):
                x_copy(t, 5 + way, e).start()
            gots[t][5 + way, own_q] = far_in[t][way][own_q]

    def relay_last(t):
        for way in range(2):
            last_copy(way, t, 1).wait_recv()
        for e in range(1, 8):
            x_copy(t, 7, e).start()
        gots[t][7, own_q] = last_in[t][own_q]

    def assemble(t, r):
        for e in range(1, 8):
            x_arrival(t, r, e).wait_recv()
        for half in range(2):
            piece = jnp.concatenate([gots[t][r, half * 4 + q] for q in range(4)], axis=0)
            mat[t, pl.ds(r * 32 + half * 16, 16), :] = piece

    def low_weights():
        @pl.loop(0, DIST)
        def _(d):
            for j in range(ACT_DEV):
                block = weights[j * DIST + d].astype(BF16)
                low_t[pl.ds(pl.multiple_of(d * SB, SB), SB), j * SB:(j + 1) * SB] = block.T

    def predict(t, c):
        rows = slice(*CHUNKS[c])
        part = jnp.dot(mat[t, rows], low_t[...], preferred_element_type=F32)
        preds[t, sens, rows] = part.astype(BF16)
        for e in range(1, 4):
            y_copy(t, c, e).start()

    def residual(t, c):
        rows = slice(*CHUNKS[c])
        for e in range(1, 4):
            y_arrival(t, c, e).wait_recv()
        total = preds[t, 0, rows].astype(F32)
        for s in range(1, 4):
            total = total + preds[t, s, rows].astype(F32)
        resid[rows] = (total - goal[t, rows]).astype(BF16)

    def gradient(t, lo, hi):
        turned = resid[lo:hi].T

        @pl.loop(0, DIST // 2)
        def _(g):
            cols = pl.ds(pl.multiple_of(g * 2 * SB, 2 * SB), 2 * SB)
            grad = jnp.dot(turned, mat[t, lo:hi, cols], preferred_element_type=F32)
            for j in range(ACT_DEV):
                for side in range(2):
                    at = j * DIST + g * 2 + side
                    scale = RATE * tab[ROW_MASK + at, samp].astype(F32)
                    weights[at] = weights[at] - scale * grad[j * SB:(j + 1) * SB, side * SB:(side + 1) * SB]

    own_loads = [pltpu.make_async_copy(slopes.at[t], grids[t][0], load_sem.at[t]) for t in range(STEPS)]
    recon_load = pltpu.make_async_copy(recon, recon_v, load_sem.at[2])
    for load in own_loads:
        load.start()
    recon_load.start()

    barrier = pltpu.get_barrier_semaphore()
    for step in (1, -1):
        pl.semaphore_signal(barrier, inc=1, device_id=z_dev(step), device_id_type=MESH)
    for e in range(1, 8):
        pl.semaphore_signal(barrier, inc=1, device_id=(sens, plane * 8 + q_of(e, 1)), device_id_type=MESH)
    for e in range(1, 4):
        pl.semaphore_signal(barrier, inc=1, device_id=((sens + e) % 4, samp), device_id_type=MESH)
    pl.semaphore_wait(barrier, 12)

    own_loads[0].wait()
    for half in range(2):
        for way in range(2):
            z_copy(way, 0, 0, half).start()
    fill_tables(act, slope, count, tab_v)
    tab_load = pltpu.make_async_copy(tab_v, tab, load_sem.at[3])
    tab_load.start()
    tab_keep = pltpu.make_async_copy(tab_v, tab_out, load_sem.at[4])
    tab_keep.start()
    own_loads[1].wait()
    tab_load.wait()
    pick(0, 0)

    recon_load.wait()

    @pl.loop(0, ACT_DEV * DIST)
    def _(at):
        weights[at] = recon_v[tab[ROW_SLOT + at, samp]] * tab[ROW_MASK + at, samp].astype(F32)

    low_weights()
    perm[...] = sample_order(plane)
    for t in range(STEPS):
        goal[t] = lax.dot_general(perm[...], targets[t], (((1,), (1,)), ((), ())),
                                  preferred_element_type=F32)

    forward(0, 0)
    forward(0, 1)
    for way in range(2):
        z_copy(way, 1, 0, 0).start()
    pick(0, 1)
    pick(0, 2)
    assemble(0, 0)
    pick_far(0)
    pick(0, 3)
    pick(0, 4)
    pass_last(0)
    for way in range(2):
        z_copy(way, 1, 0, 1).start()
    forward(1, 0)
    pick(1, 0)
    for r in range(1, 5):
        assemble(0, r)
    predict(0, 0)
    relay_far(0)
    relay_last(0)
    for r in (5, 6):
        assemble(0, r)
    predict(0, 1)
    forward(1, 1)
    assemble(0, 7)
    predict(0, 2)
    pick(1, 1)
    pick(1, 2)
    for c in range(3):
        residual(0, c)
    gradient(0, 0, SAMPLES)
    low_weights()
    assemble(1, 0)
    pick_far(1)
    pick(1, 3)
    pick(1, 4)
    pass_last(1)
    assemble(1, 1)
    assemble(1, 2)
    relay_far(1)
    assemble(1, 3)
    assemble(1, 4)
    predict(1, 0)
    relay_last(1)
    residual(1, 0)
    gradient(1, *CHUNKS[0])
    tail = CHUNKS[1][0]

    @pl.loop(0, K_MAX)
    def _(k):
        live = tab[ROW_LIVE + k, samp].astype(F32)
        base[k] = weights[tab[ROW_POS + k, samp]] * live + recon_v[k] * (1.0 - live)

    outs = [pltpu.make_async_copy(base, base_out, out_sem.at[0])]
    outs[0].start()
    assemble(1, 5)
    assemble(1, 6)
    predict(1, 1)
    assemble(1, 7)
    predict(1, 2)
    outs.append(pltpu.make_async_copy(mat.at[1, pl.ds(tail, SAMPLES - tail)], tail_out, out_sem.at[1]))
    outs[1].start()
    residual(1, 1)
    residual(1, 2)
    outs.append(tab_keep)

    for t in range(STEPS):
        for way in range(2):
            for half in range(2):
                for hop in range(2):
                    z_copy(way, t, hop, half).wait_send()
                far_copy(way, t, half).wait_send()
                last_copy(way, t, half).wait_send()
        for r in range(8):
            for e in range(1, 8):
                x_copy(t, r, e).wait_send()
        for c in range(3):
            for e in range(1, 4):
                y_copy(t, c, e).wait_send()
    for out in outs:
        out.wait()


def finish(base_in, recent, resid, tab, fitted, resid_out, base, fresh, load_sem, out_sem):
    samp = lax.axis_index("samp")
    tail = CHUNKS[1][0]
    each = K_MAX // 4

    def load(c):
        rows = pl.ds(c * each, each)
        return pltpu.make_async_copy(base_in.at[rows], base.at[rows], load_sem.at[c])

    def store(c):
        rows = pl.ds(c * each, each)
        return pltpu.make_async_copy(fresh.at[rows], fitted.at[rows], out_sem.at[c])

    for c in range(4):
        load(c).start()
    turned = resid[...].T
    resid_out[...] = jnp.dot(turned, sample_order(samp // 8), preferred_element_type=F32).astype(BF16)
    for c in range(4):
        load(c).wait()
        for k in range(c * each, (c + 1) * each):
            pos = tab[ROW_POS + k, samp]
            scale = RATE * tab[ROW_LIVE + k, samp].astype(F32)
            act = pos // DIST
            lanes = pl.ds(pl.multiple_of(act * SB, SB), SB)
            cols = pl.ds(pl.multiple_of((pos - act * DIST) * SB, SB), SB)
            grad = lax.dot_general(resid[tail:, lanes], recent[:, cols], (((0,), (0,)), ((), ())),
                                   preferred_element_type=F32)
            fresh[k] = base[k] - scale * grad
        store(c).start()
    for c in range(4):
        store(c).wait()


def per_device(slopes, targets, reconstructor, foot_act, foot_slope, foot_count):
    recon = reconstructor[0, 0]
    slopes = slopes.reshape(STEPS, LOCAL, SGB, SB).transpose(0, 2, 1, 3)
    vmem, smem, anywhere = (pl.BlockSpec(memory_space=m) for m in (pltpu.VMEM, pltpu.SMEM, pl.ANY))
    grid_set = [pltpu.VMEM((SGB, LOCAL, SB), BF16)] * 5
    pick_set = [pltpu.VMEM((8, LOCAL, WIDE), BF16)] * 5
    far_set = [[pltpu.VMEM((8, LOCAL, WIDE), BF16)] * 2] * STEPS
    last_set = [[pltpu.VMEM((4, LOCAL, WIDE), BF16)] * 2] * STEPS
    dma = pltpu.SemaphoreType.DMA
    n_samp = foot_count.shape[1]
    tail = SAMPLES - CHUNKS[1][0]
    base, recent, resid, tab = pl.pallas_call(
        kernel,
        out_shape=(jax.ShapeDtypeStruct(recon.shape, F32),
                   jax.ShapeDtypeStruct((tail, WIDE), BF16),
                   jax.ShapeDtypeStruct((SAMPLES, ACT_DEV * SB), BF16),
                   jax.ShapeDtypeStruct((TAB_ROWS, n_samp), jnp.int32)),
        in_specs=[anywhere, vmem, anywhere, vmem, vmem, vmem],
        out_specs=(anywhere, anywhere, vmem, anywhere),
        scratch_shapes=[
            pltpu.VMEM((TAB_ROWS, n_samp), jnp.int32),
            pltpu.SMEM((TAB_ROWS, n_samp), jnp.int32),
            grid_set, grid_set, pick_set, pick_set,
            far_set, far_set, last_set, last_set, [pltpu.VMEM((8, LOCAL, WIDE), BF16)] * STEPS,
            pltpu.VMEM((8, 8, LOCAL, WIDE), BF16),
            pltpu.VMEM((8, 8, LOCAL, WIDE), BF16),
            pltpu.VMEM((STEPS, SAMPLES, WIDE), BF16),
            pltpu.VMEM((ACT_DEV * DIST, SB, SB), F32),
            pltpu.VMEM((WIDE, ACT_DEV * SB), BF16),
            pltpu.VMEM((K_MAX, SB, SB), F32),
            pltpu.VMEM((K_MAX, SB, SB), F32),
            pltpu.VMEM((STEPS, 4, SAMPLES, ACT_DEV * SB), BF16),
            pltpu.VMEM((STEPS, SAMPLES, ACT_DEV * SB), F32),
            pltpu.VMEM((SAMPLES, SAMPLES), BF16),
            dma((5,)),
            dma((2, STEPS, 4, 2)), dma((2, STEPS, 4, 2)),
            dma((STEPS, 8, 8)), dma((STEPS, 8, 8)),
            dma((STEPS, 3, 3)), dma((STEPS, 3, 3)),
            dma((2,)),
        ],
        compiler_params=pltpu.CompilerParams(
            collective_id=0, has_side_effects=True, vmem_limit_bytes=40 * 1024 * 1024),
    )(slopes, targets, recon, foot_act[0].T, foot_slope[0].T, foot_count)
    fitted, fit_residual = pl.pallas_call(
        finish,
        out_shape=(jax.ShapeDtypeStruct(recon.shape, F32),
                   jax.ShapeDtypeStruct((ACT_DEV * SB, SAMPLES), BF16)),
        in_specs=[anywhere, vmem, vmem, smem],
        out_specs=(anywhere, vmem),
        scratch_shapes=[pltpu.VMEM(recon.shape, F32), pltpu.VMEM(recon.shape, F32),
                        dma((4,)), dma((4,))],
        compiler_params=pltpu.CompilerParams(vmem_limit_bytes=16 * 1024 * 1024),
    )(base, recent, resid, tab)
    return fitted[None, None], fit_residual


def solution(mesh):
    return jax.shard_map(
        per_device,
        mesh=mesh,
        in_specs=(
            P(None, "samp", "sens"),
            P(None, "samp", None),
            P("sens", "samp", None, None, None),
            P("sens", None, None),
            P("sens", None, None),
            P("sens", None),
        ),
        out_specs=(P("sens", "samp", None, None, None), P("samp", None)),
        check_vma=False,
    )
```

```python
import functools

import jax
import jax.numpy as jnp
from jax import lax
from jax.experimental import pallas as pl
from jax.experimental.pallas import tpu as pltpu
from jax.sharding import PartitionSpec as P

MESH = pl.DeviceIdType.MESH
STEPS = 2
SB = 128
SGB = 294
K_MAX = 32
DIST = 20
ACT_DEV = 2
SAMPLES = 256
LOCAL = 4
WIDE = DIST * SB
HALF = SGB // 2
RATE = K_MAX * SB / (SAMPLES + 3 * K_MAX * SB)
OFFS = (0, -1, 1, -2, 2, -3, 3, 4)
F32 = jnp.float32
BF16 = jnp.bfloat16


def place(off):
    return OFFS.index(4 if off == -4 else off)


CHUNKS = ((0, 160), (160, 224), (224, 256))
ROW_POS = 24
ROW_SLOT = ROW_POS + K_MAX
ROW_MASK = ROW_SLOT + ACT_DEV * DIST
ROW_LIVE = ROW_MASK + ACT_DEV * DIST
TAB_ROWS = ROW_LIVE + K_MAX


def fill_tables(act, slope, count, tab):
    n = slope.shape[1]
    slot = lax.broadcasted_iota(jnp.int32, (K_MAX, n), 0)
    blocks = slope[...]
    first = jnp.full((K_MAX, n), K_MAX, jnp.int32)
    for k in reversed(range(K_MAX)):
        first = jnp.where(blocks == blocks[k:k + 1], k, first)
    fresh = jnp.where(first == slot, 1, 0)
    rank = jnp.zeros((K_MAX, n), jnp.int32)
    for k in range(K_MAX):
        rank = rank + jnp.where(first > k, fresh[k:k + 1], 0)
    pos = act[...] * DIST + rank
    live = jnp.where(slot < count[...], 1, 0)
    order = lax.broadcasted_iota(jnp.int32, (ROW_POS, n), 0)
    place_of = lax.broadcasted_iota(jnp.int32, (ACT_DEV * DIST, n), 0)
    held = jnp.zeros((ROW_POS, n), jnp.int32)
    slot_of = jnp.zeros((ACT_DEV * DIST, n), jnp.int32)
    mask = jnp.zeros((ACT_DEV * DIST, n), jnp.int32)
    for k in range(K_MAX):
        held = held + jnp.where(order == rank[k:k + 1], blocks[k:k + 1] * fresh[k:k + 1], 0)
        hit = jnp.where(place_of == pos[k:k + 1], live[k:k + 1], 0)
        slot_of = slot_of + hit * k
        mask = mask + hit
    tab[0:ROW_POS, :] = held
    tab[ROW_POS:ROW_SLOT, :] = pos
    tab[ROW_SLOT:ROW_MASK, :] = slot_of
    tab[ROW_MASK:ROW_LIVE, :] = mask
    tab[ROW_LIVE:TAB_ROWS, :] = live


def sample_order(plane):
    rows = lax.broadcasted_iota(jnp.int32, (SAMPLES, SAMPLES), 0)
    cols = lax.broadcasted_iota(jnp.int32, (SAMPLES, SAMPLES), 1)
    off = jnp.zeros_like(rows)
    for r in range(8):
        off = jnp.where(rows // 32 == r, (plane + OFFS[r] + 8) % 8, off)
    return jnp.where(cols == off * 32 + rows % 32, 1.0, 0.0).astype(BF16)


def kernel(slopes, targets_in, recon, act_in, slope_in, count_in, base_out, tail_out, resid, tab_out,
           targets, act, slope, count, tab_v, tab, grid0, grid1, pick0, pick1, far_out, far_in, last_out, last_mid, last_in,
           got0, got1, mat, weights, low_t, recon_v, base,
           preds, goal, perm, load_sem, zs, zr, xs, xr, ys, yr, out_sem):
    grids, picks, gots = (grid0, grid1), (pick0, pick1), (got0, got1)
    sens = lax.axis_index("sens")
    samp = lax.axis_index("samp")
    plane = samp // 8
    col = (samp % 8) // 2
    core = samp % 2
    own_q = samp % 8

    def z_dev(step):
        return (sens, (samp + 8 * step + 64) % 64)

    def q_of(e, sign):
        return ((col + sign * (e // 2) + 4) % 4) * 2 + (core + e) % 2

    def z_copy(way, t, hop, half):
        sign = -1 if way == 0 else 1
        window = pl.ds(half * HALF, HALF)
        return pltpu.make_async_remote_copy(
            src_ref=grids[t][place(sign * hop)].at[window],
            dst_ref=grids[t][place(sign * (hop + 1))].at[window],
            send_sem=zs.at[way, t, hop, half],
            recv_sem=zr.at[way, t, hop, half],
            device_id=z_dev(-sign),
            device_id_type=MESH,
        )

    def far_copy(way, t, half):
        rows = pl.ds(half * 4, 4)
        return pltpu.make_async_remote_copy(
            src_ref=far_out[t][way].at[rows],
            dst_ref=far_in[t][way].at[rows],
            send_sem=zs.at[way, t, 2, half],
            recv_sem=zr.at[way, t, 2, half],
            device_id=z_dev(1 - 2 * way),
            device_id_type=MESH,
        )

    def last_copy(way, t, hop):
        return pltpu.make_async_remote_copy(
            src_ref=(last_out if hop == 0 else last_mid)[t][way],
            dst_ref=last_mid[t][way] if hop == 0 else last_in[t].at[pl.ds(way * 4, 4)],
            send_sem=zs.at[way, t, 3, hop],
            recv_sem=zr.at[way, t, 3, hop],
            device_id=z_dev(1 - 2 * way),
            device_id_type=MESH,
        )

    def x_source(t, r, e):
        if r < 5:
            return picks[t][r].at[e]
        return (last_in[t] if r == 7 else far_in[t][r - 5]).at[q_of(e, 1)]

    def x_copy(t, r, e):
        return pltpu.make_async_remote_copy(
            src_ref=x_source(t, r, e),
            dst_ref=gots[t].at[r, own_q],
            send_sem=xs.at[t, r, e],
            recv_sem=xr.at[t, r, e],
            device_id=(sens, plane * 8 + q_of(e, 1)),
            device_id_type=MESH,
        )

    def x_arrival(t, r, e):
        return pltpu.make_async_remote_copy(
            src_ref=x_source(t, r, e),
            dst_ref=gots[t].at[r, q_of(e, -1)],
            send_sem=xs.at[t, r, e],
            recv_sem=xr.at[t, r, e],
            device_id=(sens, plane * 8 + q_of(e, -1)),
            device_id_type=MESH,
        )

    def y_copy(t, c, e):
        rows = pl.ds(CHUNKS[c][0], CHUNKS[c][1] - CHUNKS[c][0])
        return pltpu.make_async_remote_copy(
            src_ref=preds.at[t, sens, rows],
            dst_ref=preds.at[t, sens, rows],
            send_sem=ys.at[t, c, e - 1],
            recv_sem=yr.at[t, c, e - 1],
            device_id=((sens + e) % 4, samp),
            device_id_type=MESH,
        )

    def y_arrival(t, c, e):
        other = (sens - e + 4) % 4
        rows = pl.ds(CHUNKS[c][0], CHUNKS[c][1] - CHUNKS[c][0])
        return pltpu.make_async_remote_copy(
            src_ref=preds.at[t, other, rows],
            dst_ref=preds.at[t, other, rows],
            send_sem=ys.at[t, c, e - 1],
            recv_sem=yr.at[t, c, e - 1],
            device_id=(other, samp),
            device_id_type=MESH,
        )

    def forward(t, half):
        for way in range(2):
            z_copy(way, t, 0, half).wait_recv()
            z_copy(way, t, 1, half).start()

    def pick_one(src, row, to):
        for d in range(DIST):
            to[:, d * SB:(d + 1) * SB] = src[tab[d, row]]

    def pick(t, r):
        pick_one(grids[t][r], samp, gots[t].at[r, own_q])

        @pl.loop(1, 8)
        def _(e):
            pick_one(grids[t][r], plane * 8 + q_of(e, 1), picks[t][r].at[e])

        for e in range(1, 8):
            x_copy(t, r, e).start()

    def pick_far(t):
        for half in range(2):
            for way in range(2):
                z_copy(way, t, 1, half).wait_recv()
        for way in range(2):
            ahead = (plane + 2 - 4 * way + 8) % 8 * 8 + way * 4

            @pl.loop(0, 4)
            def _(q):
                pick_one(grids[t][3 + way], ahead + q, last_out[t][way].at[q])

            last_copy(way, t, 0).start()
        for half in range(2):
            for way in range(2):
                ahead = (plane + 1 - 2 * way + 8) % 8 * 8

                @pl.loop(half * 4, half * 4 + 4)
                def _(q):
                    pick_one(grids[t][3 + way], ahead + q, far_out[t][way].at[q])

                far_copy(way, t, half).start()

    def pass_last(t):
        for way in range(2):
            last_copy(way, t, 0).wait_recv()
            last_copy(way, t, 1).start()

    def relay_far(t):
        for way in range(2):
            for half in range(2):
                far_copy(way, t, half).wait_recv()
            for e in range(1, 8):
                x_copy(t, 5 + way, e).start()
            gots[t][5 + way, own_q] = far_in[t][way][own_q]

    def relay_last(t):
        for way in range(2):
            last_copy(way, t, 1).wait_recv()
        for e in range(1, 8):
            x_copy(t, 7, e).start()
        gots[t][7, own_q] = last_in[t][own_q]

    def assemble(t, r):
        for e in range(1, 8):
            x_arrival(t, r, e).wait_recv()
        for half in range(2):
            piece = jnp.concatenate([gots[t][r, half * 4 + q] for q in range(4)], axis=0)
            mat[t, pl.ds(r * 32 + half * 16, 16), :] = piece

    def low_weights():
        @pl.loop(0, DIST)
        def _(d):
            for j in range(ACT_DEV):
                block = weights[j * DIST + d].astype(BF16)
                low_t[pl.ds(pl.multiple_of(d * SB, SB), SB), j * SB:(j + 1) * SB] = block.T

    def predict(t, c):
        rows = slice(*CHUNKS[c])
        part = jnp.dot(mat[t, rows], low_t[...], preferred_element_type=F32)
        preds[t, sens, rows] = part.astype(BF16)
        for e in range(1, 4):
            y_copy(t, c, e).start()

    def residual(t, c):
        rows = slice(*CHUNKS[c])
        for e in range(1, 4):
            y_arrival(t, c, e).wait_recv()
        total = preds[t, 0, rows].astype(F32)
        for s in range(1, 4):
            total = total + preds[t, s, rows].astype(F32)
        resid[rows] = (total - goal[t, rows]).astype(BF16)

    def gradient(t, lo, hi):
        turned = resid[lo:hi].T

        @pl.loop(0, DIST // 2)
        def _(g):
            cols = pl.ds(pl.multiple_of(g * 2 * SB, 2 * SB), 2 * SB)
            grad = jnp.dot(turned, mat[t, lo:hi, cols], preferred_element_type=F32)
            for j in range(ACT_DEV):
                for side in range(2):
                    at = j * DIST + g * 2 + side
                    scale = RATE * tab[ROW_MASK + at, samp].astype(F32)
                    weights[at] = weights[at] - scale * grad[j * SB:(j + 1) * SB, side * SB:(side + 1) * SB]

    own_loads = [pltpu.make_async_copy(slopes.at[t], grids[t][0], load_sem.at[t]) for t in range(STEPS)]
    recon_load = pltpu.make_async_copy(recon, recon_v, load_sem.at[2])
    small_loads = [pltpu.make_async_copy(src, dst, load_sem.at[5 + i]) for i, (src, dst) in enumerate(
        ((slope_in, slope), (act_in, act), (count_in, count), (targets_in, targets)))]
    own_loads[0].start()
    for load in small_loads:
        load.start()
    own_loads[1].start()
    recon_load.start()

    barrier = pltpu.get_barrier_semaphore()
    for step in (1, -1):
        pl.semaphore_signal(barrier, inc=1, device_id=z_dev(step), device_id_type=MESH)
    for e in range(1, 8):
        pl.semaphore_signal(barrier, inc=1, device_id=(sens, plane * 8 + q_of(e, 1)), device_id_type=MESH)
    for e in range(1, 4):
        pl.semaphore_signal(barrier, inc=1, device_id=((sens + e) % 4, samp), device_id_type=MESH)
    pl.semaphore_wait(barrier, 12)

    own_loads[0].wait()
    for half in range(2):
        for way in range(2):
            z_copy(way, 0, 0, half).start()
    for load in small_loads:
        load.wait()
    fill_tables(act, slope, count, tab_v)
    tab_load = pltpu.make_async_copy(tab_v, tab, load_sem.at[3])
    tab_load.start()
    tab_keep = pltpu.make_async_copy(tab_v, tab_out, load_sem.at[4])
    tab_keep.start()
    own_loads[1].wait()
    tab_load.wait()
    pick(0, 0)

    recon_load.wait()

    @pl.loop(0, ACT_DEV * DIST)
    def _(at):
        weights[at] = recon_v[tab[ROW_SLOT + at, samp]] * tab[ROW_MASK + at, samp].astype(F32)

    low_weights()
    perm[...] = sample_order(plane)
    for t in range(STEPS):
        goal[t] = lax.dot_general(perm[...], targets[t], (((1,), (1,)), ((), ())),
                                  preferred_element_type=F32)

    forward(0, 0)
    forward(0, 1)
    for way in range(2):
        z_copy(way, 1, 0, 0).start()
    pick(0, 1)
    pick(0, 2)
    assemble(0, 0)
    pick_far(0)
    pick(0, 3)
    pick(0, 4)
    pass_last(0)
    for way in range(2):
        z_copy(way, 1, 0, 1).start()
    forward(1, 0)
    pick(1, 0)
    for r in range(1, 5):
        assemble(0, r)
    predict(0, 0)
    relay_far(0)
    relay_last(0)
    for r in (5, 6):
        assemble(0, r)
    predict(0, 1)
    forward(1, 1)
    assemble(0, 7)
    predict(0, 2)
    pick(1, 1)
    pick(1, 2)
    for c in range(3):
        residual(0, c)
    gradient(0, 0, SAMPLES)
    low_weights()
    assemble(1, 0)
    pick_far(1)
    pick(1, 3)
    pick(1, 4)
    pass_last(1)
    assemble(1, 1)
    assemble(1, 2)
    relay_far(1)
    assemble(1, 3)
    assemble(1, 4)
    predict(1, 0)
    relay_last(1)
    residual(1, 0)
    gradient(1, *CHUNKS[0])
    tail = CHUNKS[1][0]

    @pl.loop(0, K_MAX)
    def _(k):
        live = tab[ROW_LIVE + k, samp].astype(F32)
        base[k] = weights[tab[ROW_POS + k, samp]] * live + recon_v[k] * (1.0 - live)

    outs = [pltpu.make_async_copy(base, base_out, out_sem.at[0])]
    outs[0].start()
    assemble(1, 5)
    assemble(1, 6)
    predict(1, 1)
    assemble(1, 7)
    predict(1, 2)
    outs.append(pltpu.make_async_copy(mat.at[1, pl.ds(tail, SAMPLES - tail)], tail_out, out_sem.at[1]))
    outs[1].start()
    residual(1, 1)
    residual(1, 2)
    outs.append(tab_keep)

    for t in range(STEPS):
        for way in range(2):
            for half in range(2):
                for hop in range(2):
                    z_copy(way, t, hop, half).wait_send()
                far_copy(way, t, half).wait_send()
                last_copy(way, t, half).wait_send()
        for r in range(8):
            for e in range(1, 8):
                x_copy(t, r, e).wait_send()
        for c in range(3):
            for e in range(1, 4):
                y_copy(t, c, e).wait_send()
    for out in outs:
        out.wait()


def finish(base_in, recent, resid, tab, fitted, resid_out, base, fresh, grad, load_sem, out_sem):
    samp = lax.axis_index("samp")
    tail = CHUNKS[1][0]
    each = K_MAX // 4

    def load(c):
        rows = pl.ds(c * each, each)
        return pltpu.make_async_copy(base_in.at[rows], base.at[rows], load_sem.at[c])

    def store(c):
        rows = pl.ds(c * each, each)
        return pltpu.make_async_copy(fresh.at[rows], fitted.at[rows], out_sem.at[c])

    for c in range(4):
        load(c).start()
    turned = resid[...].T
    late = turned[:, tail:]
    for g in range(DIST // 2):
        part = jnp.dot(late, recent[:, g * 2 * SB:(g + 1) * 2 * SB], preferred_element_type=F32)
        for j in range(ACT_DEV):
            for side in range(2):
                grad[j * DIST + g * 2 + side] = part[j * SB:(j + 1) * SB, side * SB:(side + 1) * SB]
    for c in range(4):
        load(c).wait()

        @pl.loop(c * each, (c + 1) * each)
        def _(k):
            scale = RATE * tab[ROW_LIVE + k, samp].astype(F32)
            fresh[k] = base[k] - scale * grad[tab[ROW_POS + k, samp]]

        store(c).start()
    resid_out[...] = jnp.dot(turned, sample_order(samp // 8), preferred_element_type=F32).astype(BF16)
    for c in range(4):
        store(c).wait()


def per_device(slopes, targets, reconstructor, foot_act, foot_slope, foot_count):
    recon = reconstructor[0, 0]
    slopes = slopes.reshape(STEPS, LOCAL, SGB, SB).transpose(0, 2, 1, 3)
    vmem, smem, anywhere = (pl.BlockSpec(memory_space=m) for m in (pltpu.VMEM, pltpu.SMEM, pl.ANY))
    grid_set = [pltpu.VMEM((SGB, LOCAL, SB), BF16)] * 5
    pick_set = [pltpu.VMEM((8, LOCAL, WIDE), BF16)] * 5
    far_set = [[pltpu.VMEM((8, LOCAL, WIDE), BF16)] * 2] * STEPS
    last_set = [[pltpu.VMEM((4, LOCAL, WIDE), BF16)] * 2] * STEPS
    dma = pltpu.SemaphoreType.DMA
    n_samp = foot_count.shape[1]
    tail = SAMPLES - CHUNKS[1][0]
    base, recent, resid, tab = pl.pallas_call(
        kernel,
        out_shape=(jax.ShapeDtypeStruct(recon.shape, F32),
                   jax.ShapeDtypeStruct((tail, WIDE), BF16),
                   jax.ShapeDtypeStruct((SAMPLES, ACT_DEV * SB), BF16),
                   jax.ShapeDtypeStruct((TAB_ROWS, n_samp), jnp.int32)),
        in_specs=[pl.BlockSpec(memory_space=pltpu.HBM)] * 6,
        out_specs=(anywhere, anywhere, vmem, anywhere),
        scratch_shapes=[
            pltpu.VMEM(targets.shape, BF16),
            pltpu.VMEM((K_MAX, n_samp), jnp.int32),
            pltpu.VMEM((K_MAX, n_samp), jnp.int32),
            pltpu.VMEM((1, n_samp), jnp.int32),
            pltpu.VMEM((TAB_ROWS, n_samp), jnp.int32),
            pltpu.SMEM((TAB_ROWS, n_samp), jnp.int32),
            grid_set, grid_set, pick_set, pick_set,
            far_set, far_set, last_set, last_set, [pltpu.VMEM((8, LOCAL, WIDE), BF16)] * STEPS,
            pltpu.VMEM((8, 8, LOCAL, WIDE), BF16),
            pltpu.VMEM((8, 8, LOCAL, WIDE), BF16),
            pltpu.VMEM((STEPS, SAMPLES, WIDE), BF16),
            pltpu.VMEM((ACT_DEV * DIST, SB, SB), F32),
            pltpu.VMEM((WIDE, ACT_DEV * SB), BF16),
            pltpu.VMEM((K_MAX, SB, SB), F32),
            pltpu.VMEM((K_MAX, SB, SB), F32),
            pltpu.VMEM((STEPS, 4, SAMPLES, ACT_DEV * SB), BF16),
            pltpu.VMEM((STEPS, SAMPLES, ACT_DEV * SB), F32),
            pltpu.VMEM((SAMPLES, SAMPLES), BF16),
            dma((9,)),
            dma((2, STEPS, 4, 2)), dma((2, STEPS, 4, 2)),
            dma((STEPS, 8, 8)), dma((STEPS, 8, 8)),
            dma((STEPS, 3, 3)), dma((STEPS, 3, 3)),
            dma((2,)),
        ],
        compiler_params=pltpu.CompilerParams(
            collective_id=0, has_side_effects=True, vmem_limit_bytes=40 * 1024 * 1024),
    )(*(pltpu.with_memory_space_constraint(x, pltpu.HBM) for x in (
        slopes, targets, recon, foot_act[0].T, foot_slope[0].T, foot_count)))
    fitted, fit_residual = pl.pallas_call(
        finish,
        out_shape=(jax.ShapeDtypeStruct(recon.shape, F32),
                   jax.ShapeDtypeStruct((ACT_DEV * SB, SAMPLES), BF16)),
        in_specs=[anywhere, vmem, vmem, smem],
        out_specs=(anywhere, vmem),
        scratch_shapes=[pltpu.VMEM(recon.shape, F32), pltpu.VMEM(recon.shape, F32),
                        pltpu.VMEM((ACT_DEV * DIST, SB, SB), F32),
                        dma((4,)), dma((4,))],
        compiler_params=pltpu.CompilerParams(vmem_limit_bytes=16 * 1024 * 1024),
    )(base, recent, resid, tab)
    return fitted[None, None], fit_residual


def solution(mesh):
    return jax.shard_map(
        per_device,
        mesh=mesh,
        in_specs=(
            P(None, "samp", "sens"),
            P(None, "samp", None),
            P("sens", "samp", None, None, None),
            P("sens", None, None),
            P("sens", None, None),
            P("sens", None),
        ),
        out_specs=(P("sens", "samp", None, None, None), P("samp", None)),
        check_vma=False,
    )
```

```python
import functools

import jax
import jax.numpy as jnp
from jax import lax
from jax.experimental import pallas as pl
from jax.experimental.pallas import tpu as pltpu
from jax.sharding import PartitionSpec as P

MESH = pl.DeviceIdType.MESH
STEPS = 2
SB = 128
SGB = 294
K_MAX = 32
DIST = 20
ACT_DEV = 2
SAMPLES = 256
LOCAL = 4
WIDE = DIST * SB
HALF = SGB // 2
RATE = K_MAX * SB / (SAMPLES + 3 * K_MAX * SB)
OFFS = (0, -1, 1, -2, 2, -3, 3, 4)
F32 = jnp.float32
BF16 = jnp.bfloat16


def place(off):
    return OFFS.index(4 if off == -4 else off)


CHUNKS = ((0, 96), (96, 160), (160, 224), (224, 256))
ROW_POS = 24
ROW_SLOT = ROW_POS + K_MAX
ROW_MASK = ROW_SLOT + ACT_DEV * DIST
ROW_LIVE = ROW_MASK + ACT_DEV * DIST
TAB_ROWS = ROW_LIVE + K_MAX


def fill_tables(act, slope, count, tab):
    n = slope.shape[1]
    slot = lax.broadcasted_iota(jnp.int32, (K_MAX, n), 0)
    blocks = slope[...]
    first = jnp.full((K_MAX, n), K_MAX, jnp.int32)
    for k in reversed(range(K_MAX)):
        first = jnp.where(blocks == blocks[k:k + 1], k, first)
    fresh = jnp.where(first == slot, 1, 0)
    rank = jnp.zeros((K_MAX, n), jnp.int32)
    for k in range(K_MAX):
        rank = rank + jnp.where(first > k, fresh[k:k + 1], 0)
    pos = act[...] * DIST + rank
    live = jnp.where(slot < count[...], 1, 0)
    order = lax.broadcasted_iota(jnp.int32, (ROW_POS, n), 0)
    place_of = lax.broadcasted_iota(jnp.int32, (ACT_DEV * DIST, n), 0)
    held = jnp.zeros((ROW_POS, n), jnp.int32)
    slot_of = jnp.zeros((ACT_DEV * DIST, n), jnp.int32)
    mask = jnp.zeros((ACT_DEV * DIST, n), jnp.int32)
    for k in range(K_MAX):
        held = held + jnp.where(order == rank[k:k + 1], blocks[k:k + 1] * fresh[k:k + 1], 0)
        hit = jnp.where(place_of == pos[k:k + 1], live[k:k + 1], 0)
        slot_of = slot_of + hit * k
        mask = mask + hit
    tab[0:ROW_POS, :] = held
    tab[ROW_POS:ROW_SLOT, :] = pos
    tab[ROW_SLOT:ROW_MASK, :] = slot_of
    tab[ROW_MASK:ROW_LIVE, :] = mask
    tab[ROW_LIVE:TAB_ROWS, :] = live


def sample_order(plane):
    rows = lax.broadcasted_iota(jnp.int32, (SAMPLES, SAMPLES), 0)
    cols = lax.broadcasted_iota(jnp.int32, (SAMPLES, SAMPLES), 1)
    off = jnp.zeros_like(rows)
    for r in range(8):
        off = jnp.where(rows // 32 == r, (plane + OFFS[r] + 8) % 8, off)
    return jnp.where(cols == off * 32 + rows % 32, 1.0, 0.0).astype(BF16)


def kernel(slopes, targets_in, recon, act_in, slope_in, count_in, fresh, resid_out,
           targets, act, slope, count, tab_v, tab, grid0, grid1, pick0, pick1, far_out, far_in, last_out, last_mid,
           got0, got1, mat, weights, low_t, recon_v, grad_v, resid,
           preds, goal, perm, load_sem, zs, zr, xs, xr, ys, yr):
    grids, picks, gots = (grid0, grid1), (pick0, pick1), (got0, got1)
    sens = lax.axis_index("sens")
    samp = lax.axis_index("samp")
    plane = samp // 8
    col = (samp % 8) // 2
    core = samp % 2
    own_q = samp % 8

    def z_dev(step):
        return (sens, (samp + 8 * step + 64) % 64)

    def q_of(e, sign):
        return ((col + sign * (e // 2) + 4) % 4) * 2 + (core + e) % 2

    def z_copy(way, t, hop, half):
        sign = -1 if way == 0 else 1
        window = pl.ds(half * HALF, HALF)
        return pltpu.make_async_remote_copy(
            src_ref=grids[t][place(sign * hop)].at[window],
            dst_ref=grids[t][place(sign * (hop + 1))].at[window],
            send_sem=zs.at[way, t, hop, half],
            recv_sem=zr.at[way, t, hop, half],
            device_id=z_dev(-sign),
            device_id_type=MESH,
        )

    def far_copy(way, t, half):
        rows = pl.ds(half * 4, 4)
        return pltpu.make_async_remote_copy(
            src_ref=far_out[t][way].at[rows],
            dst_ref=far_in[t][way].at[rows],
            send_sem=zs.at[way, t, 2, half],
            recv_sem=zr.at[way, t, 2, half],
            device_id=z_dev(1 - 2 * way),
            device_id_type=MESH,
        )

    def mid_copy(way, t):
        return pltpu.make_async_remote_copy(
            src_ref=last_out[t][way],
            dst_ref=last_mid[t][way],
            send_sem=zs.at[way, t, 3, 0],
            recv_sem=zr.at[way, t, 3, 0],
            device_id=z_dev(1 - 2 * way),
            device_id_type=MESH,
        )

    def last_copy(way, t, i):
        return pltpu.make_async_remote_copy(
            src_ref=last_mid[t][way].at[i],
            dst_ref=gots[t].at[7, own_q],
            send_sem=xs.at[t, 7, way * 4 + i],
            recv_sem=xr.at[t, 7, own_q],
            device_id=(sens, (plane + 1 - 2 * way + 8) % 8 * 8 + way * 4 + i),
            device_id_type=MESH,
        )

    def last_arrival(t, q):
        back = (plane - 1 + 2 * (own_q // 4) + 8) % 8
        return pltpu.make_async_remote_copy(
            src_ref=last_mid[t][0].at[0],
            dst_ref=gots[t].at[7, q],
            send_sem=xs.at[t, 7, q],
            recv_sem=xr.at[t, 7, q],
            device_id=(sens, back * 8 + q),
            device_id_type=MESH,
        )

    def x_source(t, r, e):
        if r < 5:
            return picks[t][r].at[e]
        return far_in[t][r - 5].at[q_of(e, 1)]

    def x_copy(t, r, e):
        return pltpu.make_async_remote_copy(
            src_ref=x_source(t, r, e),
            dst_ref=gots[t].at[r, own_q],
            send_sem=xs.at[t, r, e],
            recv_sem=xr.at[t, r, e],
            device_id=(sens, plane * 8 + q_of(e, 1)),
            device_id_type=MESH,
        )

    def x_arrival(t, r, e):
        return pltpu.make_async_remote_copy(
            src_ref=x_source(t, r, e),
            dst_ref=gots[t].at[r, q_of(e, -1)],
            send_sem=xs.at[t, r, e],
            recv_sem=xr.at[t, r, e],
            device_id=(sens, plane * 8 + q_of(e, -1)),
            device_id_type=MESH,
        )

    def y_copy(t, c, e):
        rows = pl.ds(CHUNKS[c][0], CHUNKS[c][1] - CHUNKS[c][0])
        return pltpu.make_async_remote_copy(
            src_ref=preds.at[t, sens, rows],
            dst_ref=preds.at[t, sens, rows],
            send_sem=ys.at[t, c, e - 1],
            recv_sem=yr.at[t, c, e - 1],
            device_id=((sens + e) % 4, samp),
            device_id_type=MESH,
        )

    def y_arrival(t, c, e):
        other = (sens - e + 4) % 4
        rows = pl.ds(CHUNKS[c][0], CHUNKS[c][1] - CHUNKS[c][0])
        return pltpu.make_async_remote_copy(
            src_ref=preds.at[t, other, rows],
            dst_ref=preds.at[t, other, rows],
            send_sem=ys.at[t, c, e - 1],
            recv_sem=yr.at[t, c, e - 1],
            device_id=(other, samp),
            device_id_type=MESH,
        )

    def forward(t, half):
        for way in range(2):
            z_copy(way, t, 0, half).wait_recv()
            z_copy(way, t, 1, half).start()

    def pick_one(src, row, to):
        for d in range(DIST):
            to[:, d * SB:(d + 1) * SB] = src[tab[d, row]]

    def pick(t, r):
        pick_one(grids[t][r], samp, gots[t].at[r, own_q])

        @pl.loop(1, 8)
        def _(e):
            pick_one(grids[t][r], plane * 8 + q_of(e, 1), picks[t][r].at[e])

        for e in range(1, 8):
            x_copy(t, r, e).start()

    def pick_far(t):
        for half in range(2):
            for way in range(2):
                z_copy(way, t, 1, half).wait_recv()
        for way in range(2):
            ahead = (plane + 2 - 4 * way + 8) % 8 * 8 + way * 4

            @pl.loop(0, 4)
            def _(q):
                pick_one(grids[t][3 + way], ahead + q, last_out[t][way].at[q])

            mid_copy(way, t).start()
        for half in range(2):
            for way in range(2):
                ahead = (plane + 1 - 2 * way + 8) % 8 * 8

                @pl.loop(half * 4, half * 4 + 4)
                def _(q):
                    pick_one(grids[t][3 + way], ahead + q, far_out[t][way].at[q])

                far_copy(way, t, half).start()

    def pass_last(t):
        for way in range(2):
            mid_copy(way, t).wait_recv()
            for i in range(4):
                last_copy(way, t, i).start()

    def relay_far(t, half):
        for way in range(2):
            far_copy(way, t, half).wait_recv()
            for q in range(half * 4, half * 4 + 4):
                e = ((q // 2 - col + 4) % 4) * 2 + (q + core) % 2

                @pl.when(own_q != q)
                def _():
                    x_copy(t, 5 + way, e).start()

            @pl.when(own_q // 4 == half)
            def _():
                gots[t][5 + way, own_q] = far_in[t][way][own_q]

    def assemble(t, r):
        for e in range(8):
            if r == 7:
                last_arrival(t, e).wait_recv()
            elif e > 0:
                x_arrival(t, r, e).wait_recv()
        for half in range(2):
            piece = jnp.concatenate([gots[t][r, half * 4 + q] for q in range(4)], axis=0)
            mat[t, pl.ds(r * 32 + half * 16, 16), :] = piece

    def low_weights():
        @pl.loop(0, DIST)
        def _(d):
            for j in range(ACT_DEV):
                block = weights[j * DIST + d].astype(BF16)
                low_t[pl.ds(pl.multiple_of(d * SB, SB), SB), j * SB:(j + 1) * SB] = block.T

    def predict(t, c):
        rows = slice(*CHUNKS[c])
        part = jnp.dot(mat[t, rows], low_t[...], preferred_element_type=F32)
        preds[t, sens, rows] = part.astype(BF16)
        for e in range(1, 4):
            y_copy(t, c, e).start()

    def residual(t, c):
        rows = slice(*CHUNKS[c])
        for e in range(1, 4):
            y_arrival(t, c, e).wait_recv()
        total = preds[t, 0, rows].astype(F32)
        for s in range(1, 4):
            total = total + preds[t, s, rows].astype(F32)
        resid[rows] = (total - goal[t, rows]).astype(BF16)

    def gradient(t, lo, hi):
        turned = resid[lo:hi].T

        @pl.loop(0, DIST // 2)
        def _(g):
            cols = pl.ds(pl.multiple_of(g * 2 * SB, 2 * SB), 2 * SB)
            grad = jnp.dot(turned, mat[t, lo:hi, cols], preferred_element_type=F32)
            for j in range(ACT_DEV):
                for side in range(2):
                    at = j * DIST + g * 2 + side
                    scale = RATE * tab[ROW_MASK + at, samp].astype(F32)
                    new = weights[at] - scale * grad[j * SB:(j + 1) * SB, side * SB:(side + 1) * SB]
                    weights[at] = new
                    if t == 0:
                        lanes = pl.ds(pl.multiple_of((g * 2 + side) * SB, SB), SB)
                        low_t[lanes, j * SB:(j + 1) * SB] = new.astype(BF16).T

    own_loads = [pltpu.make_async_copy(slopes.at[t], grids[t][0], load_sem.at[t]) for t in range(STEPS)]
    recon_load = pltpu.make_async_copy(recon, recon_v, load_sem.at[2])
    small_loads = [pltpu.make_async_copy(src, dst, load_sem.at[5 + i]) for i, (src, dst) in enumerate(
        ((slope_in, slope), (act_in, act), (count_in, count), (targets_in, targets)))]
    own_loads[0].start()
    for load in small_loads:
        load.start()
    own_loads[1].start()
    recon_load.start()

    barrier = pltpu.get_barrier_semaphore()
    for step in (1, -1):
        pl.semaphore_signal(barrier, inc=1, device_id=z_dev(step), device_id_type=MESH)
    for e in range(1, 8):
        pl.semaphore_signal(barrier, inc=1, device_id=(sens, plane * 8 + q_of(e, 1)), device_id_type=MESH)
    for e in range(1, 4):
        pl.semaphore_signal(barrier, inc=1, device_id=((sens + e) % 4, samp), device_id_type=MESH)
    for q in range(8):
        back = (plane - 1 + 2 * (own_q // 4) + 8) % 8
        pl.semaphore_signal(barrier, inc=1, device_id=(sens, back * 8 + q), device_id_type=MESH)
    pl.semaphore_wait(barrier, 20)

    own_loads[0].wait()
    for half in range(2):
        for way in range(2):
            z_copy(way, 0, 0, half).start()
    for load in small_loads:
        load.wait()
    fill_tables(act, slope, count, tab_v)
    tab_load = pltpu.make_async_copy(tab_v, tab, load_sem.at[3])
    tab_load.start()
    own_loads[1].wait()
    tab_load.wait()
    pick(0, 0)

    recon_load.wait()

    @pl.loop(0, ACT_DEV * DIST)
    def _(at):
        weights[at] = recon_v[tab[ROW_SLOT + at, samp]] * tab[ROW_MASK + at, samp].astype(F32)

    low_weights()
    perm[...] = sample_order(plane)
    for t in range(STEPS):
        goal[t] = lax.dot_general(perm[...], targets[t], (((1,), (1,)), ((), ())),
                                  preferred_element_type=F32)

    forward(0, 0)
    forward(0, 1)
    for way in range(2):
        z_copy(way, 1, 0, 0).start()
    pick(0, 1)
    pick(0, 2)
    assemble(0, 0)
    pick_far(0)
    pick(0, 3)
    pick(0, 4)
    assemble(0, 1)
    assemble(0, 2)
    predict(0, 0)
    pass_last(0)
    for way in range(2):
        z_copy(way, 1, 0, 1).start()
    forward(1, 0)
    pick(1, 0)
    relay_far(0, 0)
    assemble(0, 3)
    assemble(0, 4)
    predict(0, 1)
    relay_far(0, 1)
    residual(0, 0)
    assemble(0, 5)
    assemble(0, 6)
    predict(0, 2)
    forward(1, 1)
    assemble(0, 7)
    predict(0, 3)
    pick(1, 1)
    pick(1, 2)
    pick_far(1)
    pick(1, 3)
    pick(1, 4)
    assemble(1, 0)
    for c in range(1, 4):
        residual(0, c)
    gradient(0, 0, SAMPLES)
    pass_last(1)
    assemble(1, 1)
    assemble(1, 2)
    predict(1, 0)
    relay_far(1, 0)
    relay_far(1, 1)
    assemble(1, 3)
    assemble(1, 4)
    predict(1, 1)
    assemble(1, 5)
    assemble(1, 6)
    predict(1, 2)
    assemble(1, 7)
    predict(1, 3)
    tail = CHUNKS[3][0]
    for c in range(3):
        residual(1, c)
    gradient(1, 0, tail)

    @pl.loop(0, K_MAX)
    def _(k):
        live = tab[ROW_LIVE + k, samp].astype(F32)
        fresh[k] = weights[tab[ROW_POS + k, samp]] * live + recon_v[k] * (1.0 - live)

    residual(1, 3)
    turned = resid[...].T
    late = turned[:, tail:]
    for g in range(DIST // 2):
        part = jnp.dot(late, mat[1, tail:, g * 2 * SB:(g + 1) * 2 * SB], preferred_element_type=F32)
        for j in range(ACT_DEV):
            for side in range(2):
                grad_v[j * DIST + g * 2 + side] = part[j * SB:(j + 1) * SB, side * SB:(side + 1) * SB]
    resid_out[...] = jnp.dot(turned, perm[...], preferred_element_type=F32).astype(BF16)

    @pl.loop(0, K_MAX)
    def _(k):
        scale = RATE * tab[ROW_LIVE + k, samp].astype(F32)
        fresh[k] = fresh[k] - scale * grad_v[tab[ROW_POS + k, samp]]

    for t in range(STEPS):
        for way in range(2):
            for half in range(2):
                for hop in range(2):
                    z_copy(way, t, hop, half).wait_send()
                far_copy(way, t, half).wait_send()
            mid_copy(way, t).wait_send()
            for i in range(4):
                last_copy(way, t, i).wait_send()
        for r in range(7):
            for e in range(1, 8):
                x_copy(t, r, e).wait_send()
        for c in range(len(CHUNKS)):
            for e in range(1, 4):
                y_copy(t, c, e).wait_send()


def per_device(slopes, targets, reconstructor, foot_act, foot_slope, foot_count):
    recon = reconstructor[0, 0]
    slopes = slopes.reshape(STEPS, LOCAL, SGB, SB).transpose(0, 2, 1, 3)
    vmem = pl.BlockSpec(memory_space=pltpu.VMEM)
    grid_set = [pltpu.VMEM((SGB, LOCAL, SB), BF16)] * 5
    pick_set = [pltpu.VMEM((8, LOCAL, WIDE), BF16)] * 5
    far_set = [[pltpu.VMEM((8, LOCAL, WIDE), BF16)] * 2] * STEPS
    last_set = [[pltpu.VMEM((4, LOCAL, WIDE), BF16)] * 2] * STEPS
    dma = pltpu.SemaphoreType.DMA
    n_samp = foot_count.shape[1]
    fresh, fit_residual = pl.pallas_call(
        kernel,
        out_shape=(jax.ShapeDtypeStruct(recon.shape, F32),
                   jax.ShapeDtypeStruct((ACT_DEV * SB, SAMPLES), BF16)),
        in_specs=[pl.BlockSpec(memory_space=pltpu.HBM)] * 6,
        out_specs=(vmem, vmem),
        scratch_shapes=[
            pltpu.VMEM(targets.shape, BF16),
            pltpu.VMEM((K_MAX, n_samp), jnp.int32),
            pltpu.VMEM((K_MAX, n_samp), jnp.int32),
            pltpu.VMEM((1, n_samp), jnp.int32),
            pltpu.VMEM((TAB_ROWS, n_samp), jnp.int32),
            pltpu.SMEM((TAB_ROWS, n_samp), jnp.int32),
            grid_set, grid_set, pick_set, pick_set,
            far_set, far_set, last_set, last_set,
            pltpu.VMEM((8, 8, LOCAL, WIDE), BF16),
            pltpu.VMEM((8, 8, LOCAL, WIDE), BF16),
            pltpu.VMEM((STEPS, SAMPLES, WIDE), BF16),
            pltpu.VMEM((ACT_DEV * DIST, SB, SB), F32),
            pltpu.VMEM((WIDE, ACT_DEV * SB), BF16),
            pltpu.VMEM((K_MAX, SB, SB), F32),
            pltpu.VMEM((ACT_DEV * DIST, SB, SB), F32),
            pltpu.VMEM((SAMPLES, ACT_DEV * SB), BF16),
            pltpu.VMEM((STEPS, 4, SAMPLES, ACT_DEV * SB), BF16),
            pltpu.VMEM((STEPS, SAMPLES, ACT_DEV * SB), F32),
            pltpu.VMEM((SAMPLES, SAMPLES), BF16),
            dma((9,)),
            dma((2, STEPS, 4, 2)), dma((2, STEPS, 4, 2)),
            dma((STEPS, 8, 8)), dma((STEPS, 8, 8)),
            dma((STEPS, len(CHUNKS), 3)), dma((STEPS, len(CHUNKS), 3)),
        ],
        compiler_params=pltpu.CompilerParams(
            collective_id=0, has_side_effects=True, vmem_limit_bytes=40 * 1024 * 1024),
    )(*(pltpu.with_memory_space_constraint(x, pltpu.HBM) for x in (
        slopes, targets, recon, foot_act[0].T, foot_slope[0].T, foot_count)))
    return fresh[None, None], fit_residual


def solution(mesh):
    return jax.shard_map(
        per_device,
        mesh=mesh,
        in_specs=(
            P(None, "samp", "sens"),
            P(None, "samp", None),
            P("sens", "samp", None, None, None),
            P("sens", None, None),
            P("sens", None, None),
            P("sens", None),
        ),
        out_specs=(P("sens", "samp", None, None, None), P("samp", None)),
        check_vma=False,
    )
```

```python
import functools

import jax
import jax.numpy as jnp
from jax import lax
from jax.experimental import pallas as pl
from jax.experimental.pallas import tpu as pltpu
from jax.sharding import PartitionSpec as P

MESH = pl.DeviceIdType.MESH
STEPS = 2
SB = 128
SGB = 294
K_MAX = 32
DIST = 20
ACT_DEV = 2
SAMPLES = 256
LOCAL = 4
WIDE = DIST * SB
HALF = SGB // 2
RATE = K_MAX * SB / (SAMPLES + 3 * K_MAX * SB)
OFFS = (0, -1, 1, -2, 2, -3, 3, 4)
F32 = jnp.float32
BF16 = jnp.bfloat16


def place(off):
    return OFFS.index(4 if off == -4 else off)


CHUNKS = ((0, 96), (96, 160), (160, 256))
ROW_POS = 24
ROW_SLOT = ROW_POS + K_MAX
ROW_MASK = ROW_SLOT + ACT_DEV * DIST
ROW_LIVE = ROW_MASK + ACT_DEV * DIST
TAB_ROWS = ROW_LIVE + K_MAX


def fill_tables(act, slope, count, tab):
    n = slope.shape[1]
    slot = lax.broadcasted_iota(jnp.int32, (K_MAX, n), 0)
    blocks = slope[...]
    first = jnp.full((K_MAX, n), K_MAX, jnp.int32)
    for k in reversed(range(K_MAX)):
        first = jnp.where(blocks == blocks[k:k + 1], k, first)
    fresh = jnp.where(first == slot, 1, 0)
    rank = jnp.zeros((K_MAX, n), jnp.int32)
    for k in range(K_MAX):
        rank = rank + jnp.where(first > k, fresh[k:k + 1], 0)
    pos = act[...] * DIST + rank
    live = jnp.where(slot < count[...], 1, 0)
    order = lax.broadcasted_iota(jnp.int32, (ROW_POS, n), 0)
    place_of = lax.broadcasted_iota(jnp.int32, (ACT_DEV * DIST, n), 0)
    held = jnp.zeros((ROW_POS, n), jnp.int32)
    slot_of = jnp.zeros((ACT_DEV * DIST, n), jnp.int32)
    mask = jnp.zeros((ACT_DEV * DIST, n), jnp.int32)
    for k in range(K_MAX):
        held = held + jnp.where(order == rank[k:k + 1], blocks[k:k + 1] * fresh[k:k + 1], 0)
        hit = jnp.where(place_of == pos[k:k + 1], live[k:k + 1], 0)
        slot_of = slot_of + hit * k
        mask = mask + hit
    tab[0:ROW_POS, :] = held
    tab[ROW_POS:ROW_SLOT, :] = pos
    tab[ROW_SLOT:ROW_MASK, :] = slot_of
    tab[ROW_MASK:ROW_LIVE, :] = mask
    tab[ROW_LIVE:TAB_ROWS, :] = live


def sample_order(plane):
    rows = lax.broadcasted_iota(jnp.int32, (SAMPLES, SAMPLES), 0)
    cols = lax.broadcasted_iota(jnp.int32, (SAMPLES, SAMPLES), 1)
    off = jnp.zeros_like(rows)
    for r in range(8):
        off = jnp.where(rows // 32 == r, (plane + OFFS[r] + 8) % 8, off)
    return jnp.where(cols == off * 32 + rows % 32, 1.0, 0.0).astype(BF16)


def kernel(slopes, targets_in, recon, act_in, slope_in, count_in, fresh, resid_out,
           targets, act, slope, count, tab_v, tab, grid0, grid1, pick0, pick1, far_out, last_out, last_mid,
           got0, got1, mat, weights, low_t, recon_v, grad_v, resid,
           preds, goal, perm, load_sem, zs, zr, xs, xr, ys, yr):
    grids, picks, gots = (grid0, grid1), (pick0, pick1), (got0, got1)
    sens = lax.axis_index("sens")
    samp = lax.axis_index("samp")
    plane = samp // 8
    col = (samp % 8) // 2
    core = samp % 2
    own_q = samp % 8

    def z_dev(step):
        return (sens, (samp + 8 * step + 64) % 64)

    def q_of(e, sign):
        return ((col + sign * (e // 2) + 4) % 4) * 2 + (core + e) % 2

    def z_copy(way, t, hop, half):
        sign = -1 if way == 0 else 1
        window = pl.ds(half * HALF, HALF)
        return pltpu.make_async_remote_copy(
            src_ref=grids[t][place(sign * hop)].at[window],
            dst_ref=grids[t][place(sign * (hop + 1))].at[window],
            send_sem=zs.at[way, t, hop, half],
            recv_sem=zr.at[way, t, hop, half],
            device_id=z_dev(-sign),
            device_id_type=MESH,
        )

    def far_copy(way, t, q):
        return pltpu.make_async_remote_copy(
            src_ref=far_out[t][way].at[q],
            dst_ref=gots[t].at[5 + way, own_q],
            send_sem=xs.at[t, 5 + way, q],
            recv_sem=xr.at[t, 5 + way, own_q],
            device_id=(sens, (plane + 1 - 2 * way + 8) % 8 * 8 + q),
            device_id_type=MESH,
        )

    def far_arrival(way, t, q):
        return pltpu.make_async_remote_copy(
            src_ref=far_out[t][way].at[q],
            dst_ref=gots[t].at[5 + way, q],
            send_sem=xs.at[t, 5 + way, q],
            recv_sem=xr.at[t, 5 + way, q],
            device_id=(sens, (plane - 1 + 2 * way + 8) % 8 * 8 + q),
            device_id_type=MESH,
        )

    def mid_copy(way, t):
        return pltpu.make_async_remote_copy(
            src_ref=last_out[t][way],
            dst_ref=last_mid[t][way],
            send_sem=zs.at[way, t, 3, 0],
            recv_sem=zr.at[way, t, 3, 0],
            device_id=z_dev(1 - 2 * way),
            device_id_type=MESH,
        )

    def last_copy(way, t, i):
        return pltpu.make_async_remote_copy(
            src_ref=last_mid[t][way].at[i],
            dst_ref=gots[t].at[7, own_q],
            send_sem=xs.at[t, 7, way * 4 + i],
            recv_sem=xr.at[t, 7, own_q],
            device_id=(sens, (plane + 1 - 2 * way + 8) % 8 * 8 + way * 4 + i),
            device_id_type=MESH,
        )

    def last_arrival(t, q):
        back = (plane - 1 + 2 * (own_q // 4) + 8) % 8
        return pltpu.make_async_remote_copy(
            src_ref=last_mid[t][0].at[0],
            dst_ref=gots[t].at[7, q],
            send_sem=xs.at[t, 7, q],
            recv_sem=xr.at[t, 7, q],
            device_id=(sens, back * 8 + q),
            device_id_type=MESH,
        )

    def x_copy(t, r, e):
        return pltpu.make_async_remote_copy(
            src_ref=picks[t][r].at[e],
            dst_ref=gots[t].at[r, own_q],
            send_sem=xs.at[t, r, e],
            recv_sem=xr.at[t, r, e],
            device_id=(sens, plane * 8 + q_of(e, 1)),
            device_id_type=MESH,
        )

    def x_arrival(t, r, e):
        return pltpu.make_async_remote_copy(
            src_ref=picks[t][r].at[e],
            dst_ref=gots[t].at[r, q_of(e, -1)],
            send_sem=xs.at[t, r, e],
            recv_sem=xr.at[t, r, e],
            device_id=(sens, plane * 8 + q_of(e, -1)),
            device_id_type=MESH,
        )

    def y_copy(t, c, e):
        rows = pl.ds(CHUNKS[c][0], CHUNKS[c][1] - CHUNKS[c][0])
        return pltpu.make_async_remote_copy(
            src_ref=preds.at[t, sens, rows],
            dst_ref=preds.at[t, sens, rows],
            send_sem=ys.at[t, c, e - 1],
            recv_sem=yr.at[t, c, e - 1],
            device_id=((sens + e) % 4, samp),
            device_id_type=MESH,
        )

    def y_arrival(t, c, e):
        other = (sens - e + 4) % 4
        rows = pl.ds(CHUNKS[c][0], CHUNKS[c][1] - CHUNKS[c][0])
        return pltpu.make_async_remote_copy(
            src_ref=preds.at[t, other, rows],
            dst_ref=preds.at[t, other, rows],
            send_sem=ys.at[t, c, e - 1],
            recv_sem=yr.at[t, c, e - 1],
            device_id=(other, samp),
            device_id_type=MESH,
        )

    def forward(t, half):
        for way in range(2):
            z_copy(way, t, 0, half).wait_recv()
            z_copy(way, t, 1, half).start()

    def pick_one(src, row, to):
        for d in range(DIST):
            to[:, d * SB:(d + 1) * SB] = src[tab[d, row]]

    def pick(t, r):
        pick_one(grids[t][r], samp, gots[t].at[r, own_q])

        @pl.loop(1, 8)
        def _(e):
            pick_one(grids[t][r], plane * 8 + q_of(e, 1), picks[t][r].at[e])

            @pl.when(e > 1)
            def _():
                x_copy(t, r, e - 1).start()

        x_copy(t, r, 7).start()

    def pick_far(t):
        for half in range(2):
            for way in range(2):
                z_copy(way, t, 1, half).wait_recv()
        for way in range(2):
            ahead = (plane + 2 - 4 * way + 8) % 8 * 8 + way * 4

            @pl.loop(0, 4)
            def _(q):
                pick_one(grids[t][3 + way], ahead + q, last_out[t][way].at[q])

            mid_copy(way, t).start()
        near = [(plane + 1 - 2 * way + 8) % 8 * 8 for way in range(2)]

        @pl.loop(0, 8)
        def _(i):
            for way in range(2):
                q = (own_q + i) % 8
                pick_one(grids[t][3 + way], near[way] + q, far_out[t][way].at[q])

                @pl.when(i > 0)
                def _():
                    far_copy(way, t, (own_q + i + 7) % 8).start()

        for way in range(2):
            far_copy(way, t, (own_q + 7) % 8).start()

    def pass_last(t):
        for way in range(2):
            mid_copy(way, t).wait_recv()
            for i in range(4):
                last_copy(way, t, (own_q + i) % 4).start()

    def assemble(t, r):
        for e in range(8):
            if r == 7:
                last_arrival(t, e).wait_recv()
            elif r > 4:
                far_arrival(r - 5, t, e).wait_recv()
            elif e > 0:
                x_arrival(t, r, e).wait_recv()
        for half in range(2):
            piece = jnp.concatenate([gots[t][r, half * 4 + q] for q in range(4)], axis=0)
            mat[t, pl.ds(r * 32 + half * 16, 16), :] = piece

    def low_weights():
        @pl.loop(0, DIST)
        def _(d):
            for j in range(ACT_DEV):
                block = weights[j * DIST + d].astype(BF16)
                low_t[pl.ds(pl.multiple_of(d * SB, SB), SB), j * SB:(j + 1) * SB] = block.T

    def predict(t, c):
        rows = slice(*CHUNKS[c])
        part = jnp.dot(mat[t, rows], low_t[...], preferred_element_type=F32)
        preds[t, sens, rows] = part.astype(BF16)
        for e in range(1, 4):
            y_copy(t, c, e).start()

    def residual(t, c):
        rows = slice(*CHUNKS[c])
        for e in range(1, 4):
            y_arrival(t, c, e).wait_recv()
        total = preds[t, 0, rows].astype(F32)
        for s in range(1, 4):
            total = total + preds[t, s, rows].astype(F32)
        resid[rows] = (total - goal[t, rows]).astype(BF16)

    def gradient(t, lo, hi):
        turned = resid[lo:hi].T

        @pl.loop(0, DIST // 2)
        def _(g):
            cols = pl.ds(pl.multiple_of(g * 2 * SB, 2 * SB), 2 * SB)
            grad = jnp.dot(turned, mat[t, lo:hi, cols], preferred_element_type=F32)
            for j in range(ACT_DEV):
                for side in range(2):
                    at = j * DIST + g * 2 + side
                    scale = RATE * tab[ROW_MASK + at, samp].astype(F32)
                    new = weights[at] - scale * grad[j * SB:(j + 1) * SB, side * SB:(side + 1) * SB]
                    weights[at] = new
                    if t == 0:
                        lanes = pl.ds(pl.multiple_of((g * 2 + side) * SB, SB), SB)
                        low_t[lanes, j * SB:(j + 1) * SB] = new.astype(BF16).T

    own_loads = [pltpu.make_async_copy(slopes.at[t], grids[t][0], load_sem.at[t]) for t in range(STEPS)]
    recon_load = pltpu.make_async_copy(recon, recon_v, load_sem.at[2])
    small_loads = [pltpu.make_async_copy(src, dst, load_sem.at[5 + i]) for i, (src, dst) in enumerate(
        ((slope_in, slope), (act_in, act), (count_in, count), (targets_in, targets)))]
    own_loads[0].start()
    for load in small_loads:
        load.start()
    own_loads[1].start()
    recon_load.start()

    barrier = pltpu.get_barrier_semaphore()
    for e in range(1, 8):
        pl.semaphore_signal(barrier, inc=1, device_id=(sens, plane * 8 + q_of(e, 1)), device_id_type=MESH)
    for e in range(1, 4):
        pl.semaphore_signal(barrier, inc=1, device_id=((sens + e) % 4, samp), device_id_type=MESH)
    for step in (1, 7):
        for q in range(8):
            pl.semaphore_signal(barrier, inc=1, device_id=(sens, (plane + step) % 8 * 8 + q), device_id_type=MESH)
    pl.semaphore_wait(barrier, 26)

    own_loads[0].wait()
    for half in range(2):
        for way in range(2):
            z_copy(way, 0, 0, half).start()
    for load in small_loads:
        load.wait()
    fill_tables(act, slope, count, tab_v)
    tab_load = pltpu.make_async_copy(tab_v, tab, load_sem.at[3])
    tab_load.start()
    own_loads[1].wait()
    tab_load.wait()
    pick(0, 0)

    recon_load.wait()

    @pl.loop(0, ACT_DEV * DIST)
    def _(at):
        weights[at] = recon_v[tab[ROW_SLOT + at, samp]] * tab[ROW_MASK + at, samp].astype(F32)

    low_weights()
    perm[...] = sample_order(plane)
    for t in range(STEPS):
        goal[t] = lax.dot_general(perm[...], targets[t], (((1,), (1,)), ((), ())),
                                  preferred_element_type=F32)

    forward(0, 0)
    forward(0, 1)
    for way in range(2):
        z_copy(way, 1, 0, 0).start()
    pick(0, 1)
    pick(0, 2)
    pick_far(0)
    pick(0, 3)
    pick(0, 4)
    pass_last(0)
    for way in range(2):
        z_copy(way, 1, 0, 1).start()
    forward(1, 0)
    pick(1, 0)
    for r in range(3):
        assemble(0, r)
    predict(0, 0)
    forward(1, 1)
    pick(1, 1)
    pick(1, 2)
    assemble(0, 3)
    assemble(0, 4)
    predict(0, 1)
    for r in range(5, 8):
        assemble(0, r)
    predict(0, 2)
    pick_far(1)
    pick(1, 3)
    pick(1, 4)
    for c in range(3):
        residual(0, c)
    gradient(0, 0, SAMPLES)
    pass_last(1)
    for r in range(3):
        assemble(1, r)
    predict(1, 0)
    assemble(1, 3)
    assemble(1, 4)
    predict(1, 1)
    assemble(1, 5)
    assemble(1, 6)
    assemble(1, 7)
    predict(1, 2)
    tail = CHUNKS[2][0]
    for c in range(2):
        residual(1, c)
    gradient(1, 0, tail)

    @pl.loop(0, K_MAX // 4)
    def _(i):
        for k in (i * 4, i * 4 + 1, i * 4 + 2, i * 4 + 3):
            live = tab[ROW_LIVE + k, samp].astype(F32)
            fresh[k] = weights[tab[ROW_POS + k, samp]] * live + recon_v[k] * (1.0 - live)

    residual(1, 2)
    turned = resid[...].T
    late = turned[:, tail:]
    for g in range(DIST // 2):
        part = jnp.dot(late, mat[1, tail:, g * 2 * SB:(g + 1) * 2 * SB], preferred_element_type=F32)
        for j in range(ACT_DEV):
            for side in range(2):
                grad_v[j * DIST + g * 2 + side] = part[j * SB:(j + 1) * SB, side * SB:(side + 1) * SB]
    resid_out[...] = jnp.dot(turned, perm[...], preferred_element_type=F32).astype(BF16)

    @pl.loop(0, K_MAX // 4)
    def _(i):
        for k in (i * 4, i * 4 + 1, i * 4 + 2, i * 4 + 3):
            scale = RATE * tab[ROW_LIVE + k, samp].astype(F32)
            fresh[k] = fresh[k] - scale * grad_v[tab[ROW_POS + k, samp]]

    for t in range(STEPS):
        for way in range(2):
            for half in range(2):
                for hop in range(2):
                    z_copy(way, t, hop, half).wait_send()
            mid_copy(way, t).wait_send()
            for q in range(8):
                far_copy(way, t, q).wait_send()
            for i in range(4):
                last_copy(way, t, i).wait_send()
        for r in range(5):
            for e in range(1, 8):
                x_copy(t, r, e).wait_send()
        for c in range(len(CHUNKS)):
            for e in range(1, 4):
                y_copy(t, c, e).wait_send()


def per_device(slopes, targets, reconstructor, foot_act, foot_slope, foot_count):
    recon = reconstructor[0, 0]
    slopes = slopes.reshape(STEPS, LOCAL, SGB, SB).transpose(0, 2, 1, 3)
    vmem = pl.BlockSpec(memory_space=pltpu.VMEM)
    grid_set = [pltpu.VMEM((SGB, LOCAL, SB), BF16)] * 5
    pick_set = [pltpu.VMEM((8, LOCAL, WIDE), BF16)] * 5
    far_set = [[pltpu.VMEM((8, LOCAL, WIDE), BF16)] * 2] * STEPS
    last_set = [[pltpu.VMEM((4, LOCAL, WIDE), BF16)] * 2] * STEPS
    dma = pltpu.SemaphoreType.DMA
    n_samp = foot_count.shape[1]
    fresh, fit_residual = pl.pallas_call(
        kernel,
        out_shape=(jax.ShapeDtypeStruct(recon.shape, F32),
                   jax.ShapeDtypeStruct((ACT_DEV * SB, SAMPLES), BF16)),
        in_specs=[pl.BlockSpec(memory_space=pltpu.HBM)] * 6,
        out_specs=(vmem, vmem),
        scratch_shapes=[
            pltpu.VMEM(targets.shape, BF16),
            pltpu.VMEM((K_MAX, n_samp), jnp.int32),
            pltpu.VMEM((K_MAX, n_samp), jnp.int32),
            pltpu.VMEM((1, n_samp), jnp.int32),
            pltpu.VMEM((TAB_ROWS, n_samp), jnp.int32),
            pltpu.SMEM((TAB_ROWS, n_samp), jnp.int32),
            grid_set, grid_set, pick_set, pick_set,
            far_set, last_set, last_set,
            pltpu.VMEM((8, 8, LOCAL, WIDE), BF16),
            pltpu.VMEM((8, 8, LOCAL, WIDE), BF16),
            pltpu.VMEM((STEPS, SAMPLES, WIDE), BF16),
            pltpu.VMEM((ACT_DEV * DIST, SB, SB), F32),
            pltpu.VMEM((WIDE, ACT_DEV * SB), BF16),
            pltpu.VMEM((K_MAX, SB, SB), F32),
            pltpu.VMEM((ACT_DEV * DIST, SB, SB), F32),
            pltpu.VMEM((SAMPLES, ACT_DEV * SB), BF16),
            pltpu.VMEM((STEPS, 4, SAMPLES, ACT_DEV * SB), BF16),
            pltpu.VMEM((STEPS, SAMPLES, ACT_DEV * SB), F32),
            pltpu.VMEM((SAMPLES, SAMPLES), BF16),
            dma((9,)),
            dma((2, STEPS, 4, 2)), dma((2, STEPS, 4, 2)),
            dma((STEPS, 8, 8)), dma((STEPS, 8, 8)),
            dma((STEPS, len(CHUNKS), 3)), dma((STEPS, len(CHUNKS), 3)),
        ],
        compiler_params=pltpu.CompilerParams(
            collective_id=0, has_side_effects=True, vmem_limit_bytes=40 * 1024 * 1024),
    )(*(pltpu.with_memory_space_constraint(x, pltpu.HBM) for x in (
        slopes, targets, recon, foot_act[0].T, foot_slope[0].T, foot_count)))
    return fresh[None, None], fit_residual


def solution(mesh):
    return jax.shard_map(
        per_device,
        mesh=mesh,
        in_specs=(
            P(None, "samp", "sens"),
            P(None, "samp", None),
            P("sens", "samp", None, None, None),
            P("sens", None, None),
            P("sens", None, None),
            P("sens", None),
        ),
        out_specs=(P("sens", "samp", None, None, None), P("samp", None)),
        check_vma=False,
    )
```

```python
import functools

import jax
import jax.numpy as jnp
from jax import lax
from jax.experimental import pallas as pl
from jax.experimental.pallas import tpu as pltpu
from jax.sharding import PartitionSpec as P

MESH = pl.DeviceIdType.MESH
STEPS = 2
SB = 128
SGB = 294
K_MAX = 32
DIST = 20
ACT_DEV = 2
SAMPLES = 256
LOCAL = 4
WIDE = DIST * SB
HALF = SGB // 2
RATE = K_MAX * SB / (SAMPLES + 3 * K_MAX * SB)
OFFS = (0, -1, 1, -2, 2, -3, 3, 4)
F32 = jnp.float32
BF16 = jnp.bfloat16


def place(off):
    return OFFS.index(4 if off == -4 else off)


CHUNKS = ((0, 96), (96, 160), (160, 256))
ROW_POS = 24
ROW_SLOT = ROW_POS + K_MAX
ROW_MASK = ROW_SLOT + ACT_DEV * DIST
ROW_LIVE = ROW_MASK + ACT_DEV * DIST
TAB_ROWS = ROW_LIVE + K_MAX


def fill_tables(act, slope, count, tab):
    n = slope.shape[1]
    slot = lax.broadcasted_iota(jnp.int32, (K_MAX, n), 0)
    blocks = slope[...]
    first = jnp.full((K_MAX, n), K_MAX, jnp.int32)
    for k in reversed(range(K_MAX)):
        first = jnp.where(blocks == blocks[k:k + 1], k, first)
    fresh = jnp.where(first == slot, 1, 0)
    rank = jnp.zeros((K_MAX, n), jnp.int32)
    for k in range(K_MAX):
        rank = rank + jnp.where(first > k, fresh[k:k + 1], 0)
    pos = act[...] * DIST + rank
    live = jnp.where(slot < count[...], 1, 0)
    order = lax.broadcasted_iota(jnp.int32, (ROW_POS, n), 0)
    place_of = lax.broadcasted_iota(jnp.int32, (ACT_DEV * DIST, n), 0)
    held = jnp.zeros((ROW_POS, n), jnp.int32)
    slot_of = jnp.zeros((ACT_DEV * DIST, n), jnp.int32)
    mask = jnp.zeros((ACT_DEV * DIST, n), jnp.int32)
    for k in range(K_MAX):
        held = held + jnp.where(order == rank[k:k + 1], blocks[k:k + 1] * fresh[k:k + 1], 0)
        hit = jnp.where(place_of == pos[k:k + 1], live[k:k + 1], 0)
        slot_of = slot_of + hit * k
        mask = mask + hit
    tab[0:ROW_POS, :] = held
    tab[ROW_POS:ROW_SLOT, :] = pos
    tab[ROW_SLOT:ROW_MASK, :] = slot_of
    tab[ROW_MASK:ROW_LIVE, :] = mask
    tab[ROW_LIVE:TAB_ROWS, :] = live


def sample_order(plane):
    rows = lax.broadcasted_iota(jnp.int32, (SAMPLES, SAMPLES), 0)
    cols = lax.broadcasted_iota(jnp.int32, (SAMPLES, SAMPLES), 1)
    off = jnp.zeros_like(rows)
    for r in range(8):
        off = jnp.where(rows // 32 == r, (plane + OFFS[r] + 8) % 8, off)
    return jnp.where(cols == off * 32 + rows % 32, 1.0, 0.0).astype(BF16)


def kernel(slopes, targets_in, recon, act_in, slope_in, count_in, fresh, resid_out,
           targets, act, slope, count, tab_v, tab, grid0, grid1, pick0, pick1, far_out, last_out, last_mid,
           got0, got1, mat, weights, low_t, recon_v, grad_v, resid,
           preds, goal, perm, load_sem, zs, zr, xs, xr, ys, yr):
    grids, picks, gots = (grid0, grid1), (pick0, pick1), (got0, got1)
    sens = lax.axis_index("sens")
    samp = lax.axis_index("samp")
    plane = samp // 8
    col = (samp % 8) // 2
    core = samp % 2
    own_q = samp % 8

    def z_dev(step):
        return (sens, (samp + 8 * step + 64) % 64)

    def q_of(e, sign):
        return ((col + sign * (e // 2) + 4) % 4) * 2 + (core + e) % 2

    def z_copy(way, t, hop, half):
        sign = -1 if way == 0 else 1
        window = pl.ds(half * HALF, HALF)
        return pltpu.make_async_remote_copy(
            src_ref=grids[t][place(sign * hop)].at[window],
            dst_ref=grids[t][place(sign * (hop + 1))].at[window],
            send_sem=zs.at[way, t, hop, half],
            recv_sem=zr.at[way, t, hop, half],
            device_id=z_dev(-sign),
            device_id_type=MESH,
        )

    def far_copy(way, t, q):
        return pltpu.make_async_remote_copy(
            src_ref=far_out[t][way].at[q],
            dst_ref=gots[t].at[5 + way, own_q],
            send_sem=xs.at[t, 5 + way, q],
            recv_sem=xr.at[t, 5 + way, own_q],
            device_id=(sens, (plane + 1 - 2 * way + 8) % 8 * 8 + q),
            device_id_type=MESH,
        )

    def far_arrival(way, t, q):
        return pltpu.make_async_remote_copy(
            src_ref=far_out[t][way].at[q],
            dst_ref=gots[t].at[5 + way, q],
            send_sem=xs.at[t, 5 + way, q],
            recv_sem=xr.at[t, 5 + way, q],
            device_id=(sens, (plane - 1 + 2 * way + 8) % 8 * 8 + q),
            device_id_type=MESH,
        )

    def mid_copy(way, t):
        return pltpu.make_async_remote_copy(
            src_ref=last_out[t][way],
            dst_ref=last_mid[t][way],
            send_sem=zs.at[way, t, 3, 0],
            recv_sem=zr.at[way, t, 3, 0],
            device_id=z_dev(1 - 2 * way),
            device_id_type=MESH,
        )

    def last_copy(way, t, i):
        return pltpu.make_async_remote_copy(
            src_ref=last_mid[t][way].at[i],
            dst_ref=gots[t].at[7, own_q],
            send_sem=xs.at[t, 7, way * 4 + i],
            recv_sem=xr.at[t, 7, own_q],
            device_id=(sens, (plane + 1 - 2 * way + 8) % 8 * 8 + way * 4 + i),
            device_id_type=MESH,
        )

    def last_arrival(t, q):
        back = (plane - 1 + 2 * (own_q // 4) + 8) % 8
        return pltpu.make_async_remote_copy(
            src_ref=last_mid[t][0].at[0],
            dst_ref=gots[t].at[7, q],
            send_sem=xs.at[t, 7, q],
            recv_sem=xr.at[t, 7, q],
            device_id=(sens, back * 8 + q),
            device_id_type=MESH,
        )

    def x_copy(t, r, e):
        return pltpu.make_async_remote_copy(
            src_ref=picks[t][r].at[e],
            dst_ref=gots[t].at[r, own_q],
            send_sem=xs.at[t, r, e],
            recv_sem=xr.at[t, r, e],
            device_id=(sens, plane * 8 + q_of(e, 1)),
            device_id_type=MESH,
        )

    def x_arrival(t, r, e):
        return pltpu.make_async_remote_copy(
            src_ref=picks[t][r].at[e],
            dst_ref=gots[t].at[r, q_of(e, -1)],
            send_sem=xs.at[t, r, e],
            recv_sem=xr.at[t, r, e],
            device_id=(sens, plane * 8 + q_of(e, -1)),
            device_id_type=MESH,
        )

    def y_copy(t, c, e):
        rows = pl.ds(CHUNKS[c][0], CHUNKS[c][1] - CHUNKS[c][0])
        return pltpu.make_async_remote_copy(
            src_ref=preds.at[t, sens, rows],
            dst_ref=preds.at[t, sens, rows],
            send_sem=ys.at[t, c, e - 1],
            recv_sem=yr.at[t, c, e - 1],
            device_id=((sens + e) % 4, samp),
            device_id_type=MESH,
        )

    def y_arrival(t, c, e):
        other = (sens - e + 4) % 4
        rows = pl.ds(CHUNKS[c][0], CHUNKS[c][1] - CHUNKS[c][0])
        return pltpu.make_async_remote_copy(
            src_ref=preds.at[t, other, rows],
            dst_ref=preds.at[t, other, rows],
            send_sem=ys.at[t, c, e - 1],
            recv_sem=yr.at[t, c, e - 1],
            device_id=(other, samp),
            device_id_type=MESH,
        )

    def forward(t, half):
        for way in range(2):
            z_copy(way, t, 0, half).wait_recv()
            z_copy(way, t, 1, half).start()

    def pick_one(src, row, to):
        for d in range(DIST):
            to[:, d * SB:(d + 1) * SB] = src[tab[d, row]]

    def pick(t, r):
        pick_one(grids[t][r], samp, gots[t].at[r, own_q])

        @pl.loop(1, 8)
        def _(e):
            pick_one(grids[t][r], plane * 8 + q_of(e, 1), picks[t][r].at[e])

            @pl.when(e > 1)
            def _():
                x_copy(t, r, e - 1).start()

        x_copy(t, r, 7).start()

    def pick_far(t):
        for half in range(2):
            for way in range(2):
                z_copy(way, t, 1, half).wait_recv()
        for way in range(2):
            ahead = (plane + 2 - 4 * way + 8) % 8 * 8 + way * 4

            @pl.loop(0, 4)
            def _(q):
                pick_one(grids[t][3 + way], ahead + q, last_out[t][way].at[q])

            mid_copy(way, t).start()
        near = [(plane + 1 - 2 * way + 8) % 8 * 8 for way in range(2)]

        @pl.loop(0, 8)
        def _(i):
            for way in range(2):
                q = (own_q + i) % 8
                pick_one(grids[t][3 + way], near[way] + q, far_out[t][way].at[q])

                @pl.when(i > 0)
                def _():
                    far_copy(way, t, (own_q + i + 7) % 8).start()

        for way in range(2):
            far_copy(way, t, (own_q + 7) % 8).start()

    def pass_last(t):
        for way in range(2):
            mid_copy(way, t).wait_recv()
            for i in range(4):
                last_copy(way, t, (own_q + i) % 4).start()

    def assemble(t, r):
        for e in range(8):
            if r == 7:
                last_arrival(t, e).wait_recv()
            elif r > 4:
                far_arrival(r - 5, t, e).wait_recv()
            elif e > 0:
                x_arrival(t, r, e).wait_recv()
        for half in range(2):
            piece = jnp.concatenate([gots[t][r, half * 4 + q] for q in range(4)], axis=0)
            mat[t, pl.ds(r * 32 + half * 16, 16), :] = piece

    def low_weights():
        @pl.loop(0, DIST)
        def _(d):
            for j in range(ACT_DEV):
                block = weights[j * DIST + d].astype(BF16)
                low_t[pl.ds(pl.multiple_of(d * SB, SB), SB), j * SB:(j + 1) * SB] = block.T

    def predict(t, c):
        rows = slice(*CHUNKS[c])
        part = jnp.dot(mat[t, rows], low_t[...], preferred_element_type=F32)
        preds[t, sens, rows] = part.astype(BF16)
        for e in (2, 1, 3):
            y_copy(t, c, e).start()

    def residual(t, c):
        rows = slice(*CHUNKS[c])
        for e in range(1, 4):
            y_arrival(t, c, e).wait_recv()
        total = preds[t, 0, rows].astype(F32)
        for s in range(1, 4):
            total = total + preds[t, s, rows].astype(F32)
        resid[rows] = (total - goal[t, rows]).astype(BF16)

    def gradient(t, lo, hi):
        turned = resid[lo:hi].T

        @pl.loop(0, DIST // 2)
        def _(g):
            cols = pl.ds(pl.multiple_of(g * 2 * SB, 2 * SB), 2 * SB)
            grad = jnp.dot(turned, mat[t, lo:hi, cols], preferred_element_type=F32)
            for j in range(ACT_DEV):
                for side in range(2):
                    at = j * DIST + g * 2 + side
                    scale = RATE * tab[ROW_MASK + at, samp].astype(F32)
                    new = weights[at] - scale * grad[j * SB:(j + 1) * SB, side * SB:(side + 1) * SB]
                    weights[at] = new
                    if t == 0:
                        lanes = pl.ds(pl.multiple_of((g * 2 + side) * SB, SB), SB)
                        low_t[lanes, j * SB:(j + 1) * SB] = new.astype(BF16).T

    own_loads = [pltpu.make_async_copy(slopes.at[t], grids[t][0], load_sem.at[t]) for t in range(STEPS)]
    recon_load = pltpu.make_async_copy(recon, recon_v, load_sem.at[2])
    small_loads = [pltpu.make_async_copy(src, dst, load_sem.at[5 + i]) for i, (src, dst) in enumerate(
        ((slope_in, slope), (act_in, act), (count_in, count), (targets_in, targets)))]
    own_loads[0].start()
    for load in small_loads:
        load.start()
    own_loads[1].start()
    recon_load.start()

    barrier = pltpu.get_barrier_semaphore()
    for e in range(1, 8):
        pl.semaphore_signal(barrier, inc=1, device_id=(sens, plane * 8 + q_of(e, 1)), device_id_type=MESH)
    for e in range(1, 4):
        pl.semaphore_signal(barrier, inc=1, device_id=((sens + e) % 4, samp), device_id_type=MESH)
    for step in (1, 7):
        for q in range(8):
            pl.semaphore_signal(barrier, inc=1, device_id=(sens, (plane + step) % 8 * 8 + q), device_id_type=MESH)
    pl.semaphore_wait(barrier, 26)

    own_loads[0].wait()
    for half in range(2):
        for way in range(2):
            z_copy(way, 0, 0, half).start()
    for load in small_loads:
        load.wait()
    fill_tables(act, slope, count, tab_v)
    tab_load = pltpu.make_async_copy(tab_v, tab, load_sem.at[3])
    tab_load.start()
    own_loads[1].wait()
    tab_load.wait()
    pick(0, 0)

    recon_load.wait()

    @pl.loop(0, ACT_DEV * DIST)
    def _(at):
        weights[at] = recon_v[tab[ROW_SLOT + at, samp]] * tab[ROW_MASK + at, samp].astype(F32)

    low_weights()
    perm[...] = sample_order(plane)
    for t in range(STEPS):
        goal[t] = lax.dot_general(perm[...], targets[t], (((1,), (1,)), ((), ())),
                                  preferred_element_type=F32)

    forward(0, 0)
    forward(0, 1)
    for way in range(2):
        z_copy(way, 1, 0, 0).start()
    pick(0, 1)
    pick(0, 2)
    pick_far(0)
    pick(0, 3)
    pick(0, 4)
    pass_last(0)
    for way in range(2):
        z_copy(way, 1, 0, 1).start()
    forward(1, 0)
    pick(1, 0)
    for r in range(3):
        assemble(0, r)
    predict(0, 0)
    forward(1, 1)
    pick(1, 1)
    pick(1, 2)
    assemble(0, 3)
    assemble(0, 4)
    predict(0, 1)
    for r in range(5, 8):
        assemble(0, r)
    predict(0, 2)
    pick_far(1)
    pick(1, 3)
    pick(1, 4)
    for c in range(3):
        residual(0, c)
    gradient(0, 0, SAMPLES)
    pass_last(1)
    for r in range(3):
        assemble(1, r)
    predict(1, 0)
    assemble(1, 3)
    assemble(1, 4)
    predict(1, 1)
    assemble(1, 5)
    assemble(1, 6)
    assemble(1, 7)
    predict(1, 2)
    tail = CHUNKS[2][0]
    for c in range(2):
        residual(1, c)
    gradient(1, 0, tail)

    @pl.loop(0, K_MAX // 4)
    def _(i):
        for k in (i * 4, i * 4 + 1, i * 4 + 2, i * 4 + 3):
            live = tab[ROW_LIVE + k, samp].astype(F32)
            fresh[k] = weights[tab[ROW_POS + k, samp]] * live + recon_v[k] * (1.0 - live)

    residual(1, 2)
    turned = resid[...].T
    late = turned[:, tail:]
    for g in range(DIST // 2):
        part = jnp.dot(late, mat[1, tail:, g * 2 * SB:(g + 1) * 2 * SB], preferred_element_type=F32)
        for j in range(ACT_DEV):
            for side in range(2):
                grad_v[j * DIST + g * 2 + side] = part[j * SB:(j + 1) * SB, side * SB:(side + 1) * SB]
    resid_out[...] = jnp.dot(turned, perm[...], preferred_element_type=F32).astype(BF16)

    @pl.loop(0, K_MAX // 4)
    def _(i):
        for k in (i * 4, i * 4 + 1, i * 4 + 2, i * 4 + 3):
            scale = RATE * tab[ROW_LIVE + k, samp].astype(F32)
            fresh[k] = fresh[k] - scale * grad_v[tab[ROW_POS + k, samp]]

    for t in range(STEPS):
        for way in range(2):
            for half in range(2):
                for hop in range(2):
                    z_copy(way, t, hop, half).wait_send()
            mid_copy(way, t).wait_send()
            for q in range(8):
                far_copy(way, t, q).wait_send()
            for i in range(4):
                last_copy(way, t, i).wait_send()
        for r in range(5):
            for e in range(1, 8):
                x_copy(t, r, e).wait_send()
        for c in range(len(CHUNKS)):
            for e in range(1, 4):
                y_copy(t, c, e).wait_send()


def per_device(slopes, targets, reconstructor, foot_act, foot_slope, foot_count):
    recon = reconstructor[0, 0]
    slopes = slopes.reshape(STEPS, LOCAL, SGB, SB).transpose(0, 2, 1, 3)
    vmem = pl.BlockSpec(memory_space=pltpu.VMEM)
    grid_set = [pltpu.VMEM((SGB, LOCAL, SB), BF16)] * 5
    pick_set = [pltpu.VMEM((8, LOCAL, WIDE), BF16)] * 5
    far_set = [[pltpu.VMEM((8, LOCAL, WIDE), BF16)] * 2] * STEPS
    last_set = [[pltpu.VMEM((4, LOCAL, WIDE), BF16)] * 2] * STEPS
    dma = pltpu.SemaphoreType.DMA
    n_samp = foot_count.shape[1]
    fresh, fit_residual = pl.pallas_call(
        kernel,
        out_shape=(jax.ShapeDtypeStruct(recon.shape, F32),
                   jax.ShapeDtypeStruct((ACT_DEV * SB, SAMPLES), BF16)),
        in_specs=[pl.BlockSpec(memory_space=pltpu.HBM)] * 6,
        out_specs=(vmem, vmem),
        scratch_shapes=[
            pltpu.VMEM(targets.shape, BF16),
            pltpu.VMEM((K_MAX, n_samp), jnp.int32),
            pltpu.VMEM((K_MAX, n_samp), jnp.int32),
            pltpu.VMEM((1, n_samp), jnp.int32),
            pltpu.VMEM((TAB_ROWS, n_samp), jnp.int32),
            pltpu.SMEM((TAB_ROWS, n_samp), jnp.int32),
            grid_set, grid_set, pick_set, pick_set,
            far_set, last_set, last_set,
            pltpu.VMEM((8, 8, LOCAL, WIDE), BF16),
            pltpu.VMEM((8, 8, LOCAL, WIDE), BF16),
            pltpu.VMEM((STEPS, SAMPLES, WIDE), BF16),
            pltpu.VMEM((ACT_DEV * DIST, SB, SB), F32),
            pltpu.VMEM((WIDE, ACT_DEV * SB), BF16),
            pltpu.VMEM((K_MAX, SB, SB), F32),
            pltpu.VMEM((ACT_DEV * DIST, SB, SB), F32),
            pltpu.VMEM((SAMPLES, ACT_DEV * SB), BF16),
            pltpu.VMEM((STEPS, 4, SAMPLES, ACT_DEV * SB), BF16),
            pltpu.VMEM((STEPS, SAMPLES, ACT_DEV * SB), F32),
            pltpu.VMEM((SAMPLES, SAMPLES), BF16),
            dma((9,)),
            dma((2, STEPS, 4, 2)), dma((2, STEPS, 4, 2)),
            dma((STEPS, 8, 8)), dma((STEPS, 8, 8)),
            dma((STEPS, len(CHUNKS), 3)), dma((STEPS, len(CHUNKS), 3)),
        ],
        compiler_params=pltpu.CompilerParams(
            collective_id=0, has_side_effects=True, vmem_limit_bytes=40 * 1024 * 1024),
    )(*(pltpu.with_memory_space_constraint(x, pltpu.HBM) for x in (
        slopes, targets, recon, foot_act[0].T, foot_slope[0].T, foot_count)))
    return fresh[None, None], fit_residual


def solution(mesh):
    return jax.shard_map(
        per_device,
        mesh=mesh,
        in_specs=(
            P(None, "samp", "sens"),
            P(None, "samp", None),
            P("sens", "samp", None, None, None),
            P("sens", None, None),
            P("sens", None, None),
            P("sens", None),
        ),
        out_specs=(P("sens", "samp", None, None, None), P("samp", None)),
        check_vma=False,
    )
```
